256 devices in a mesh: section: 16 (over y_hi, x, core), tensor: 16 (over y_lo, z).
Axes of the slice: x: 4, y: 4 (y_hi: 2, y_lo: 2; y = y_hi * 2 + y_lo), z: 8, core: 2. Of those that a mesh axis runs over, the one named last changes fastest.
Arguments:
- state: bfloat16 [16, 256, 6144], P('section', None, 'tensor'), may hold values from -6 to 6
- ln_gain: float32 [16, 6144], P('section'), may hold values from 0.1 to 1.9
- w_qkv: bfloat16 [16, 6144, 3, 4096], P('section', None, None, 'tensor'), may hold values from -0.078125 to 0.078125
- qk_gain: float32 [16, 2, 128], P('section'), may hold values from 0.5 to 1.5
- w_out: bfloat16 [16, 4096, 6144], P('section', 'tensor'), may hold values from -1 to 1
Outputs:
- advanced: bfloat16 [16, 256, 6144], P('section', None, 'tensor')
The draws below stay inside these ranges and needn't reach their ends.
All inputs are finite; a program needn't handle non-finite values.
Results may differ from the reference program's by a relative error of at most 0.03.
Values may be sent and summed in bfloat16 or wider, within the bound.
No kernel may reach another device: no remote copies, remote signals or barrier semaphores. Data moves between devices by JAX's collectives and lax.ppermute only.
A program may use at most 128 MiB of HBM per device.

```python
import jax
import jax.numpy as jnp
from jax import lax

D = 6144
HEADS = 32
HD = 128
PATCHES = 256
STEPS = 2
SECTIONS = 16


def with_spikes(result, key, source, target, parts, factor):
    owner, partner = [(jnp.arange(result.shape[axis_at]) // (result.shape[axis_at] // parts)).reshape([-1 if axis == axis_at else 1 for axis in range(result.ndim)]) for axis_at in (source, target)]
    chosen = jax.random.permutation(key, parts)[partner]
    strong = (owner == chosen) | (owner == (partner + parts // 2) % parts)
    return jnp.where(strong, factor * result, result)


def level_of(key, dims, cuts, low, largest):
    factor_of = 1.0
    for position, shards_of in cuts:
        draws = jax.random.uniform(jax.random.fold_in(jax.random.fold_in(key, 6), position), (shards_of,), jnp.float32, low / len(cuts), largest / len(cuts))
        factor_of = factor_of * jnp.repeat(jnp.exp(draws), dims[position] // shards_of).reshape((-1,) + (1,) * (len(dims) - 1 - position))
    return factor_of


def gaussian(rng, dims, scale, reach, cuts=(), kind=jnp.bfloat16):
    drawn = jax.random.normal(rng, dims, jnp.float32) * scale
    if len(cuts) > 0:
        drawn = level_of(rng, dims, cuts, -0.22, 0.18) * drawn
    return jnp.clip(drawn, min=-reach, max=reach).astype(kind)


def gaussian_with(key, extent, scale, bound, split, heavy, dtype=jnp.bfloat16):
    array = scale * jax.random.normal(key, extent, jnp.float32)
    if split:
        array = array * level_of(key, extent, split, -0.22, 0.18)
    return jnp.clip(with_spikes(array, jax.random.fold_in(key, 3), *heavy), -bound, bound).astype(dtype)


def setup_inputs(seed: int = 0) -> dict:
    key_list = jax.random.split(jax.random.key(seed), 6)
    return {
        "state": gaussian(key_list[0], (SECTIONS, PATCHES, D), 1.0, 6.0, ((0, 16), (2, 16))),
        "ln_gain": jnp.clip(1.0 + 0.18 * jax.random.normal(key_list[1], (SECTIONS, D), jnp.float32), 0.1, 1.9),
        "w_qkv": gaussian(key_list[2], (SECTIONS, D, 3, HEADS * HD), D ** -0.5, 0.078125, ((0, 16), (3, 16))),
        "qk_gain": jnp.clip(1.0 + 0.1 * jax.random.normal(key_list[3], (SECTIONS, 2, HD), jnp.float32), 0.5, 1.5),
        "w_out": gaussian_with(key_list[4], (SECTIONS, HEADS * HD, D), (HEADS * HD // 64) ** -0.5, 1.0, ((0, 16), (1, 16)), (1, 2, 16, 2.0)),
    }


def layer_norm(values, gain):
    mean = lax.optimization_barrier(jnp.mean(values, axis=-1, keepdims=True))
    squares = lax.optimization_barrier(jnp.mean(values * values, axis=-1, keepdims=True))
    spread = squares - mean * mean
    return (values - mean) * lax.rsqrt(spread + 1e-06) * gain

def one_block(current, gain_row, qkv_weight, norm_gains, out_weight):
    patches = current.shape[0]
    normed = layer_norm(current.astype(jnp.float32), gain_row).astype(jnp.bfloat16)
    projected = jnp.dot(normed, qkv_weight.reshape(D, 3 * HEADS * HD), preferred_element_type=jnp.float32)
    projected = projected.reshape(patches, 3, HEADS, HD)
    query = layer_norm(projected[:, 0], norm_gains[0]).astype(jnp.bfloat16)
    keys_all = layer_norm(projected[:, 1], norm_gains[1]).astype(jnp.bfloat16)
    value = projected[:, 2].astype(jnp.bfloat16)
    scores = jnp.einsum('phe,qhe->hpq', query.astype(jnp.float32), keys_all.astype(jnp.float32)) / jnp.sqrt(jnp.float32(HD))
    expo = jnp.exp(scores)
    attend = (expo / lax.optimization_barrier(jnp.sum(expo, axis=-1, keepdims=True))).astype(jnp.bfloat16)
    mixed_rows = jnp.einsum('hpq,qhe->phe', attend.astype(jnp.float32), value.astype(jnp.float32))
    mixed_rows = mixed_rows.astype(jnp.bfloat16).reshape(patches, HEADS * HD)
    branch = jnp.dot(mixed_rows, out_weight, preferred_element_type=jnp.float32)
    return (current.astype(jnp.float32) + branch).astype(jnp.bfloat16)

def reference(state, ln_gain, w_qkv, qk_gain, w_out):
    current = state
    for step_index in range(STEPS):
        renewed = lax.map(lambda items: one_block(*items), (current, ln_gain, w_qkv, qk_gain, w_out))
        current = jnp.roll(renewed, 1, axis=0)
    return current
```

```python
import functools

import jax
import jax.numpy as jnp
from jax import lax
from jax.experimental import pallas as pl
from jax.experimental.pallas import tpu as pltpu
from jax.sharding import Mesh, PartitionSpec as P

HD = 128
STEPS = 2
SECTION = ("yh", "x", "core")
PAIR = "yl"
RING = "z"


def attention_block(
    pieces, local_heads, rows_ref, gain_ref, qk_gain_ref, w_hbm, *refs
):
    x_refs, (out_ref, w_ref, normed_ref, w_sem) = refs[:pieces], refs[pieces:]
    patches, width = x_refs[0].shape
    full_width = pieces * width

    def fetch(at):
        start = pl.multiple_of(rows_ref[at] * width, width)
        return pltpu.make_async_copy(
            w_hbm.at[:, pl.ds(start, width), :],
            w_ref.at[:, pl.ds(at * width, width), :],
            w_sem.at[at],
        )

    for at in range(pieces):
        fetch(at).start()

    total = jnp.zeros((patches, 128), jnp.float32)
    squares = jnp.zeros((patches, 128), jnp.float32)
    for x_ref in x_refs:
        for lane in range(0, width, 128):
            part = x_ref[:, lane : lane + 128].astype(jnp.float32)
            total += part
            squares += part * part
    mean = jnp.sum(total, axis=-1, keepdims=True) / full_width
    spread = jnp.sum(squares, axis=-1, keepdims=True) / full_width - mean * mean
    scale = lax.rsqrt(spread + 1e-06)
    for at, x_ref in enumerate(x_refs):
        values = x_ref[...].astype(jnp.float32)
        gain = gain_ref[rows_ref[at]]
        normed_ref[:, at * width : (at + 1) * width] = ((values - mean) * scale * gain).astype(jnp.bfloat16)
    for at in range(pieces):
        fetch(at).wait()

    normed = normed_ref[...]

    def head_norm(values, gain):
        mean = jnp.mean(values, axis=-1, keepdims=True)
        squares = jnp.mean(values * values, axis=-1, keepdims=True)
        return ((values - mean) * lax.rsqrt(squares - mean * mean + 1e-06) * gain).astype(jnp.bfloat16)

    query, keys, value = (jnp.dot(normed, w_ref[at], preferred_element_type=jnp.float32) for at in range(3))
    for head in range(local_heads):
        cols = slice(head * HD, (head + 1) * HD)
        q = head_norm(query[:, cols], qk_gain_ref[0:1, :])
        k = head_norm(keys[:, cols], qk_gain_ref[1:2, :])
        v = value[:, cols].astype(jnp.bfloat16)
        scores = lax.dot_general(q, k, (((1,), (1,)), ((), ())), preferred_element_type=jnp.float32)
        expo = jnp.exp(scores / (HD**0.5))
        attend = (expo / jnp.sum(expo, axis=-1, keepdims=True)).astype(jnp.bfloat16)
        out_ref[:, cols] = jnp.dot(attend, v, preferred_element_type=jnp.float32).astype(jnp.bfloat16)


def attention(pieces, rows, gain, qk_gain, w_qkv):
    patches, width = pieces[0].shape
    count = len(pieces)
    cols = w_qkv.shape[2]
    vmem = pl.BlockSpec(memory_space=pltpu.VMEM)
    return pl.pallas_call(
        functools.partial(attention_block, count, cols // HD),
        out_shape=jax.ShapeDtypeStruct((patches, cols), jnp.bfloat16),
        in_specs=[pl.BlockSpec(memory_space=pltpu.SMEM), vmem, vmem, pl.BlockSpec(memory_space=pl.ANY)]
        + [vmem] * count,
        out_specs=vmem,
        scratch_shapes=[
            pltpu.VMEM((3, count * width, cols), jnp.bfloat16),
            pltpu.VMEM((patches, count * width), jnp.bfloat16),
            pltpu.SemaphoreType.DMA((count,)),
        ],
        compiler_params=pltpu.CompilerParams(vmem_limit_bytes=40 << 20),
        name="attention_block",
    )(rows, gain, qk_gain, w_qkv, *pieces)


def projection_block(order_ref, own_ref, other_ref, w_own_ref, w_other_ref, *out_refs):
    own, other = own_ref[...], other_ref[...]
    for at, out_ref in enumerate(out_refs):
        here = order_ref[at]
        out = jnp.dot(own, w_own_ref[here], preferred_element_type=jnp.float32)
        out += jnp.dot(other, w_other_ref[here], preferred_element_type=jnp.float32)
        out_ref[...] = out.astype(out_ref.dtype)


def projection(order, own, other, w_own, w_other):
    patches = own.shape[0]
    ring, _, width = w_own.shape
    vmem = pl.BlockSpec(memory_space=pltpu.VMEM)
    return pl.pallas_call(
        projection_block,
        out_shape=[jax.ShapeDtypeStruct((patches, width), jnp.bfloat16)] * ring,
        in_specs=[pl.BlockSpec(memory_space=pltpu.SMEM)] + [vmem] * 4,
        out_specs=[vmem] * ring,
        compiler_params=pltpu.CompilerParams(vmem_limit_bytes=24 << 20),
        name="projection_block",
    )(order, own, other, w_own, w_other)


def shifted(block, axis, by):
    peers = lax.axis_size(axis)
    return lax.ppermute(block, axis, [(i, (i + by) % peers) for i in range(peers)])


def to_next_section(block, across):
    sections = lax.axis_size(SECTION)
    pairs = [
        (2 * s + y, 2 * ((s + 1) % sections) + (1 - y if across else y)) for s in range(sections) for y in range(2)
    ]
    return lax.ppermute(block, SECTION + (PAIR,), pairs)


def on_device(state, ln_gain, w_qkv, qk_gain, w_out):
    ring = lax.axis_size(RING)
    half = ring // 2
    here, side = lax.axis_index(RING), lax.axis_index(PAIR)
    own = state[0]
    width = own.shape[1]
    heads_cols = w_qkv.shape[3]
    w_planes = jnp.transpose(w_qkv[0], (1, 0, 2))
    gain = ln_gain[0].reshape(2 * ring, 1, width)

    offsets = [0] + [o for k in range(half) for o in ((-k - 1, k + 1) if k < half - 1 else (-k - 1,))]
    rows = jnp.stack([(side ^ y) * ring + (here + o) % ring for o in offsets for y in (0, 1)]).astype(jnp.int32)
    order = ((here + jnp.arange(ring)) % ring).astype(jnp.int32)

    other = shifted(own, PAIR, 1)

    w_split = jnp.transpose(w_out[0].reshape(heads_cols, 2, ring, width), (1, 2, 0, 3))
    w_own = lax.dynamic_index_in_dim(w_split, side, 0, keepdims=False)
    w_send = lax.dynamic_index_in_dim(w_split, 1 - side, 0, keepdims=False)
    w_send, other = lax.optimization_barrier((w_send, other))
    w_other = shifted(w_send, PAIR, 1)

    for step_index in range(STEPS):
        pieces = [own, other]
        ahead, back = [own, other], [own, other]
        for k in range(half):
            ahead = [shifted(block, RING, 1) for block in ahead]
            pieces += ahead
            if k < half - 1:
                back = [shifted(block, RING, -1) for block in back]
                pieces += back
        mixed = attention(pieces, rows, gain, qk_gain[0], w_planes)
        mixed_other = shifted(mixed, PAIR, 1)
        parts = projection(order, mixed, mixed_other, w_own, w_other)

        def plus(block, at):
            return (block.astype(jnp.float32) + parts[at % ring].astype(jnp.float32)).astype(jnp.bfloat16)

        ahead, back = parts[half], parts[ring - half + 1]
        for k in range(half):
            ahead = shifted(ahead, RING, 1)
            if k < half - 1:
                ahead = plus(ahead, half - 1 - k)
                back = shifted(back, RING, -1)
                if k < half - 2:
                    back = plus(back, -(half - 2 - k))
        branch = ahead.astype(jnp.float32) + back.astype(jnp.float32) + parts[0].astype(jnp.float32)
        renewed = (own.astype(jnp.float32) + branch).astype(jnp.bfloat16)
        own = to_next_section(renewed, False)
        if step_index < STEPS - 1:
            other = to_next_section(renewed, True)
    return own[None]


def solution(mesh):
    sizes = dict(mesh.shape)
    assert sizes == {"section": 16, "tensor": 16}
    devices = mesh.devices.reshape(2, 4, 2, 2, 8)
    fine = Mesh(devices, SECTION + (PAIR, RING))
    tensor = (PAIR, RING)
    return jax.shard_map(
        on_device,
        mesh=fine,
        in_specs=(
            P(SECTION, None, tensor),
            P(SECTION, None),
            P(SECTION, None, None, tensor),
            P(SECTION, None, None),
            P(SECTION, tensor, None),
        ),
        out_specs=P(SECTION, None, tensor),
        check_vma=False,
    )
```

```python
import functools

import jax
import jax.numpy as jnp
from jax import lax
from jax.experimental import pallas as pl
from jax.experimental.pallas import tpu as pltpu
from jax.sharding import Mesh, PartitionSpec as P

HD = 128
STEPS = 2
EPS = 1e-06
SECTION = ("yh", "x", "core")
PAIR = "yl"
RING = "z"
EXTRA = 16
VMEM = pl.BlockSpec(memory_space=pltpu.VMEM)
SMEM = pl.BlockSpec(memory_space=pltpu.SMEM)
ROWS = 64


def add_blocks(first, rows_ref, gain_ref, w_hbm, x_refs, acc_ref, sums_ref, shift_ref, scaled_ref, w_ref, w_sem):
    patches, width = x_refs[0].shape

    def fetch(at):
        start = pl.multiple_of(rows_ref[at] * width, width)
        return pltpu.make_async_copy(
            w_hbm.at[:, pl.ds(start, width), :], w_ref.at[:, pl.ds(at * width, width), :], w_sem.at[at]
        )

    for at in range(len(x_refs)):
        fetch(at).start()
    for at in range(len(x_refs)):
        gain = gain_ref[rows_ref[at]]
        high = gain.astype(jnp.bfloat16).astype(jnp.float32)
        row = lax.broadcasted_iota(jnp.int32, (EXTRA, width), 0)
        both = jnp.where(row == 0, high, jnp.where(row == 1, gain - high, 0.0))
        scaled_ref[patches : patches + EXTRA, at * width : (at + 1) * width] = both.astype(jnp.bfloat16)

    @pl.loop(0, patches // ROWS)
    def _(block):
        part = pl.ds(pl.multiple_of(block * ROWS, ROWS), ROWS)
        if first:
            shift = jnp.sum(x_refs[0][part, :].astype(jnp.float32), axis=-1, keepdims=True) / width
            shift_ref[part, :] = jnp.broadcast_to(shift, (ROWS, 128))
            total = squares = jnp.zeros((ROWS, 128), jnp.float32)
        else:
            shift = shift_ref[part, 0:1]
            total, squares = sums_ref[0, part, :], sums_ref[1, part, :]
        for at, x_ref in enumerate(x_refs):
            values = x_ref[part, :].astype(jnp.float32)
            for lane in range(0, width, 128):
                piece = values[:, lane : lane + 128]
                total += piece
                squares += piece * piece
            scaled = (values - shift) * gain_ref[rows_ref[at]]
            scaled_ref[part, at * width : (at + 1) * width] = scaled.astype(jnp.bfloat16)
        sums_ref[0, part, :] = total
        sums_ref[1, part, :] = squares

    for at in range(len(x_refs)):
        fetch(at).wait()

    @pl.loop(0, 3)
    def _(plane):
        out = jnp.dot(scaled_ref[...], w_ref[plane], preferred_element_type=jnp.float32)
        if first:
            acc_ref[plane] = out
        else:
            acc_ref[plane] += out


def partial_block(first, blocks, rows_ref, gain_ref, w_hbm, *refs):
    x_refs, refs = refs[:blocks], refs[blocks:]
    if not first:
        refs = refs[3:]
    acc_ref, sums_ref, shift_ref, scaled_ref, w_ref, w_sem = refs
    add_blocks(first, rows_ref, gain_ref, w_hbm, x_refs, acc_ref, sums_ref, shift_ref, scaled_ref, w_ref, w_sem)


def final_block(blocks, pieces, rows_ref, gain_ref, w_hbm, *refs):
    x_refs, (acc_in, sums_in, shift_ref, qk_gain_ref, out_ref, acc_ref, sums_ref, scaled_ref, w_ref, w_sem) = (
        refs[:blocks],
        refs[blocks:],
    )
    patches, width = x_refs[0].shape
    full_width = pieces * width
    acc_ref[...] = acc_in[...]
    sums_ref[...] = sums_in[...]
    add_blocks(False, rows_ref, gain_ref, w_hbm, x_refs, acc_ref, sums_ref, shift_ref, scaled_ref, w_ref, w_sem)

    mean = jnp.sum(sums_ref[0], axis=-1, keepdims=True) / full_width
    spread = jnp.sum(sums_ref[1], axis=-1, keepdims=True) / full_width - mean * mean
    scale = lax.rsqrt(spread + EPS)
    offset = mean - shift_ref[:, 0:1]

    def projected(plane, cols):
        out = acc_ref[plane, 0:patches, cols]
        weighed = acc_ref[plane, patches : patches + 1, cols] + acc_ref[plane, patches + 1 : patches + 2, cols]
        return (out - offset * weighed) * scale

    def head_norm(values, gain):
        mean = jnp.mean(values, axis=-1, keepdims=True)
        squares = jnp.mean(values * values, axis=-1, keepdims=True)
        return ((values - mean) * lax.rsqrt(squares - mean * mean + EPS) * gain).astype(jnp.bfloat16)

    for head in range(out_ref.shape[1] // HD):
        cols = slice(head * HD, (head + 1) * HD)
        query = head_norm(projected(0, cols), qk_gain_ref[0:1, :])
        keys = head_norm(projected(1, cols), qk_gain_ref[1:2, :])
        value = projected(2, cols).astype(jnp.bfloat16)
        scores = lax.dot_general(query, keys, (((1,), (1,)), ((), ())), preferred_element_type=jnp.float32)
        expo = jnp.exp(scores / (HD**0.5))
        attend = (expo / jnp.sum(expo, axis=-1, keepdims=True)).astype(jnp.bfloat16)
        out_ref[:, cols] = jnp.dot(attend, value, preferred_element_type=jnp.float32).astype(jnp.bfloat16)


def scratch(blocks, patches, width, cols):
    return [
        pltpu.VMEM((patches + EXTRA, blocks * width), jnp.bfloat16),
        pltpu.VMEM((3, blocks * width, cols), jnp.bfloat16),
        pltpu.SemaphoreType.DMA((blocks,)),
    ]


def sums_of(patches, cols):
    return [
        ((3, patches + EXTRA, cols), jnp.float32),
        ((2, patches, 128), jnp.float32),
        ((patches, 128), jnp.float32),
    ]


def partial(rows, gain, w_planes, blocks, carried):
    patches, width = blocks[0].shape
    cols = w_planes.shape[2]
    first = carried is None
    count = len(blocks)
    carried = [] if first else list(carried)
    return pl.pallas_call(
        functools.partial(partial_block, first, count),
        out_shape=[jax.ShapeDtypeStruct(*s) for s in sums_of(patches, cols)],
        in_specs=[SMEM, VMEM, pl.BlockSpec(memory_space=pltpu.HBM)] + [VMEM] * (count + len(carried)),
        out_specs=[VMEM] * 3,
        input_output_aliases={} if first else {3 + count + i: i for i in range(3)},
        scratch_shapes=scratch(count, patches, width, cols),
        compiler_params=pltpu.CompilerParams(vmem_limit_bytes=24 << 20),
        name="qkv_first" if first else "qkv_more",
    )(rows, gain, w_planes, *blocks, *carried)


def attention(rows, gain, w_planes, blocks, carried, qk_gain, pieces):
    patches, width = blocks[0].shape
    cols = w_planes.shape[2]
    count = len(blocks)
    acc, sums, _ = sums_of(patches, cols)
    return pl.pallas_call(
        functools.partial(final_block, count, pieces),
        out_shape=jax.ShapeDtypeStruct((patches, cols), jnp.bfloat16),
        in_specs=[SMEM, VMEM, pl.BlockSpec(memory_space=pltpu.HBM)] + [VMEM] * (count + 4),
        out_specs=VMEM,
        scratch_shapes=[pltpu.VMEM(*acc), pltpu.VMEM(*sums)] + scratch(count, patches, width, cols),
        compiler_params=pltpu.CompilerParams(vmem_limit_bytes=32 << 20),
        name="attention_block",
    )(rows, gain, w_planes, *blocks, *carried, qk_gain)


def projection_block(order_ref, own_ref, other_ref, w_own_ref, w_other_ref, *out_refs):
    ring, width = len(out_refs), out_refs[0].shape[1]
    for at, out_ref in enumerate(out_refs):
        in_own = pl.ds(pl.multiple_of((order_ref[ring] + order_ref[at]) * width, width), width)
        in_other = pl.ds(pl.multiple_of(order_ref[at] * width, width), width)
        out = jnp.dot(own_ref[...], w_own_ref[:, in_own], preferred_element_type=jnp.float32)
        out += jnp.dot(other_ref[...], w_other_ref[:, in_other], preferred_element_type=jnp.float32)
        out_ref[...] = out.astype(out_ref.dtype)


def projection(order, own, other, w_own, w_other, ring):
    shape = (own.shape[0], w_other.shape[1] // ring)
    return pl.pallas_call(
        projection_block,
        out_shape=[jax.ShapeDtypeStruct(shape, jnp.bfloat16)] * ring,
        in_specs=[SMEM] + [VMEM] * 4,
        out_specs=[VMEM] * ring,
        compiler_params=pltpu.CompilerParams(vmem_limit_bytes=24 << 20),
        name="projection_block",
    )(order, own, other, w_own, w_other)


def shifted(block, axis, by):
    peers = lax.axis_size(axis)
    return lax.ppermute(block, axis, [(i, (i + by) % peers) for i in range(peers)])


def across(block, by):
    ring = lax.axis_size(RING)
    pairs = [(y * ring + z, (1 - y) * ring + (z + by) % ring) for y in range(2) for z in range(ring)]
    return lax.ppermute(block, (PAIR, RING), pairs)


def to_next_section(block, by):
    sections, ring = lax.axis_size(SECTION), lax.axis_size(RING)

    def place(s, y, z):
        return ((s % sections) * 2 + y) * ring + z % ring

    pairs = [
        (place(s, y, z), place(s + 1, y, z + by)) for s in range(sections) for y in range(2) for z in range(ring)
    ]
    return lax.ppermute(block, SECTION + (PAIR, RING), pairs)


def added(*blocks):
    return functools.reduce(jnp.add, (b.astype(jnp.float32) for b in blocks)).astype(jnp.bfloat16)


def on_device(state, ln_gain, w_qkv, qk_gain, w_out):
    ring = lax.axis_size(RING)
    assert ring == 8
    here, side = lax.axis_index(RING), lax.axis_index(PAIR)
    own = state[0]
    width = own.shape[1]
    w_planes = pltpu.with_memory_space_constraint(jnp.transpose(w_qkv[0], (1, 0, 2)), pltpu.HBM)
    gain = ln_gain[0].reshape(2 * ring, 1, width)
    w_own = w_out[0]

    def rows(*places):
        return jnp.stack([(side ^ y) * ring + (here + o) % ring for y, o in places]).astype(jnp.int32)

    rows_of = [
        rows((0, 0), (1, 0), (0, -1), (0, 1)),
        rows((0, -2), (0, 2), (1, -1), (1, 1)),
        rows((0, -3), (0, 3), (1, -2), (1, 2)),
        rows((0, -4), (1, -3), (1, 3), (1, 4)),
    ]
    order = jnp.append((here + jnp.arange(ring)) % ring, side * ring).astype(jnp.int32)

    half = w_own.shape[1] // 2
    w_send = lax.dynamic_slice_in_dim(w_own, (1 - side) * half, half, 1)
    w_other = None
    for step_index in range(STEPS):
        a_up, a_down = shifted(own, RING, 1), shifted(own, RING, -1)
        other = shifted(own, PAIR, 1)
        a_up, a_down, other = lax.optimization_barrier((a_up, a_down, other))
        blocks = [[own, other, a_up, a_down]]
        b_up = b_down = other
        for _ in range(2):
            a_up, a_down = shifted(a_up, RING, 1), shifted(a_down, RING, -1)
            b_up, b_down = shifted(b_up, RING, 1), shifted(b_down, RING, -1)
            blocks.append([a_up, a_down, b_up, b_down])
            if w_other is None:
                w_send = lax.optimization_barrier((w_send, a_up, a_down, b_up, b_down))[0]
                w_other = shifted(w_send, PAIR, 1)
        blocks.append([shifted(a_up, RING, 1), shifted(b_up, RING, 1), shifted(b_down, RING, -1), across(a_down, -1)])

        carried = None
        for at in range(3):
            carried = partial(rows_of[at], gain, w_planes, blocks[at], carried)
        mixed = attention(rows_of[3], gain, w_planes, blocks[3], carried, qk_gain[0], 2 * ring)
        parts = projection(order, mixed, shifted(mixed, PAIR, 1), w_own, w_other, ring)

        up, down = parts[4], parts[5]
        for k in (3, 2, 1):
            up = added(shifted(up, RING, 1), parts[k])
            down = shifted(down, RING, -1)
            if k > 1:
                down = added(down, parts[9 - k])
        last = added(own, down, parts[0])
        own = added(to_next_section(last, 0), to_next_section(up, 1))
    return own[None]


def solution(mesh):
    assert dict(mesh.shape) == {"section": 16, "tensor": 16}
    devices = mesh.devices.reshape(2, 4, 2, 2, 8)
    fine = Mesh(devices, SECTION + (PAIR, RING))
    tensor = (PAIR, RING)
    return jax.shard_map(
        on_device,
        mesh=fine,
        in_specs=(
            P(SECTION, None, tensor),
            P(SECTION, None),
            P(SECTION, None, None, tensor),
            P(SECTION, None, None),
            P(SECTION, tensor, None),
        ),
        out_specs=P(SECTION, None, tensor),
        check_vma=False,
    )
```

```python
import functools

import jax
import jax.numpy as jnp
from jax import lax
from jax.experimental import pallas as pl
from jax.experimental.pallas import tpu as pltpu
from jax.sharding import Mesh, PartitionSpec as P

HD = 128
STEPS = 2
EPS = 1e-06
SECTION = ("yh", "x", "core")
PAIR = "yl"
RING = "z"
EXTRA = 16
VMEM = pl.BlockSpec(memory_space=pltpu.VMEM)
SMEM = pl.BlockSpec(memory_space=pltpu.SMEM)
ROWS = 64
GROUP = 4
LATE = 4


def fetches(rows_ref, w_hbm, w_ref, w_sem, count, width):
    def fetch(at):
        start = pl.multiple_of(rows_ref[at] * width, width)
        return pltpu.make_async_copy(
            w_hbm.at[:, pl.ds(start, width), :], w_ref.at[:, pl.ds(at * width, width), :], w_sem.at[at]
        )

    return [fetch(at) for at in range(count)]


def scale_blocks(first, rows_ref, gain_ref, x_refs, before_ref, sums_ref, shift_ref, scaled_ref):
    patches, width = x_refs[0].shape
    for at in range(len(x_refs)):
        gain = gain_ref[rows_ref[at]]
        high = gain.astype(jnp.bfloat16).astype(jnp.float32)
        row = lax.broadcasted_iota(jnp.int32, (EXTRA, width), 0)
        both = jnp.where(row == 0, high, jnp.where(row == 1, gain - high, 0.0))
        scaled_ref[patches : patches + EXTRA, at * width : (at + 1) * width] = both.astype(jnp.bfloat16)

    @pl.loop(0, patches // ROWS)
    def _(block):
        part = pl.ds(pl.multiple_of(block * ROWS, ROWS), ROWS)
        if first:
            shift = jnp.sum(x_refs[0][part, :].astype(jnp.float32), axis=-1, keepdims=True) / width
            shift_ref[part, :] = jnp.broadcast_to(shift, (ROWS, 128))
            total = squares = jnp.zeros((ROWS, 128), jnp.float32)
        else:
            shift = shift_ref[part, 0:1]
            total, squares = before_ref[0, part, :], before_ref[1, part, :]
        for at, x_ref in enumerate(x_refs):
            values = x_ref[part, :].astype(jnp.float32)
            for lane in range(0, width, 128):
                piece = values[:, lane : lane + 128]
                total += piece
                squares += piece * piece
            scaled = (values - shift) * gain_ref[rows_ref[at]]
            scaled_ref[part, at * width : (at + 1) * width] = scaled.astype(jnp.bfloat16)
        sums_ref[0, part, :] = total
        sums_ref[1, part, :] = squares


def partial_block(blocks, rows_ref, late_rows_ref, gain_ref, w_hbm, *refs):
    x_refs, (acc_ref, sums_ref, shift_ref, w_late_ref, scaled_ref, w_ref, w_sem, late_sem) = refs[:blocks], refs[blocks:]
    width = x_refs[0].shape[1]
    now = fetches(rows_ref, w_hbm, w_ref, w_sem, blocks, width)
    late = fetches(late_rows_ref, w_hbm, w_late_ref, late_sem, LATE, width)
    for copy in now + late:
        copy.start()
    scale_blocks(True, rows_ref, gain_ref, x_refs, None, sums_ref, shift_ref, scaled_ref)
    for copy in now:
        copy.wait()
    depth = GROUP * width

    @pl.loop(0, 3)
    def _(plane):
        for group in range(blocks // GROUP):
            span = slice(group * depth, (group + 1) * depth)
            out = jnp.dot(scaled_ref[:, span], w_ref[plane, span, :], preferred_element_type=jnp.float32)
            if group == 0:
                acc_ref[plane] = out
            else:
                acc_ref[plane] += out

    for copy in late:
        copy.wait()


def final_block(blocks, pieces, rows_ref, gain_ref, *refs):
    x_refs, (acc_ref, before_ref, shift_ref, w_ref, qk_gain_ref, out_ref, sums_ref, scaled_ref) = (
        refs[:blocks],
        refs[blocks:],
    )
    patches, width = x_refs[0].shape
    full_width = pieces * width
    scale_blocks(False, rows_ref, gain_ref, x_refs, before_ref, sums_ref, shift_ref, scaled_ref)
    mean = jnp.sum(sums_ref[0], axis=-1, keepdims=True) / full_width
    spread = jnp.sum(sums_ref[1], axis=-1, keepdims=True) / full_width - mean * mean
    scale = lax.rsqrt(spread + EPS)
    offset = mean - shift_ref[:, 0:1]

    def projected(plane):
        out = acc_ref[plane] + jnp.dot(scaled_ref[...], w_ref[plane], preferred_element_type=jnp.float32)
        weighed = out[patches : patches + 1] + out[patches + 1 : patches + 2]
        return (out[:patches] - offset * weighed) * scale

    def head_norm(values, gain):
        mean = jnp.mean(values, axis=-1, keepdims=True)
        squares = jnp.mean(values * values, axis=-1, keepdims=True)
        return ((values - mean) * lax.rsqrt(squares - mean * mean + EPS) * gain).astype(jnp.bfloat16)

    all_query, all_keys, all_value = (projected(plane) for plane in range(3))
    for head in range(out_ref.shape[1] // HD):
        cols = slice(head * HD, (head + 1) * HD)
        query = head_norm(all_query[:, cols], qk_gain_ref[0:1, :])
        keys = head_norm(all_keys[:, cols], qk_gain_ref[1:2, :])
        value = all_value[:, cols].astype(jnp.bfloat16)
        scores = lax.dot_general(query, keys, (((1,), (1,)), ((), ())), preferred_element_type=jnp.float32)
        expo = jnp.exp(scores * HD**-0.5)
        attend = (expo * (1.0 / jnp.sum(expo, axis=-1, keepdims=True))).astype(jnp.bfloat16)
        out_ref[:, cols] = jnp.dot(attend, value, preferred_element_type=jnp.float32).astype(jnp.bfloat16)


def partial(rows, late_rows, gain, w_planes, blocks):
    patches, width = blocks[0].shape
    planes, _, cols = w_planes.shape
    count = len(blocks)
    return pl.pallas_call(
        functools.partial(partial_block, count),
        out_shape=[
            jax.ShapeDtypeStruct((planes, patches + EXTRA, cols), jnp.float32),
            jax.ShapeDtypeStruct((2, patches, 128), jnp.float32),
            jax.ShapeDtypeStruct((patches, 128), jnp.float32),
            jax.ShapeDtypeStruct((planes, LATE * width, cols), jnp.bfloat16),
        ],
        in_specs=[SMEM, SMEM, VMEM, pl.BlockSpec(memory_space=pltpu.HBM)] + [VMEM] * count,
        out_specs=[VMEM] * 4,
        scratch_shapes=[
            pltpu.VMEM((patches + EXTRA, count * width), jnp.bfloat16),
            pltpu.VMEM((planes, count * width, cols), jnp.bfloat16),
            pltpu.SemaphoreType.DMA((count,)),
            pltpu.SemaphoreType.DMA((LATE,)),
        ],
        compiler_params=pltpu.CompilerParams(vmem_limit_bytes=28 << 20),
        name="qkv_partial",
    )(rows, late_rows, gain, w_planes, *blocks)


def attention(rows, gain, blocks, carried, qk_gain, pieces):
    patches, width = blocks[0].shape
    cols = carried[0].shape[2]
    count = len(blocks)
    return pl.pallas_call(
        functools.partial(final_block, count, pieces),
        out_shape=jax.ShapeDtypeStruct((patches, cols), jnp.bfloat16),
        in_specs=[SMEM] + [VMEM] * (count + 6),
        out_specs=VMEM,
        scratch_shapes=[
            pltpu.VMEM((2, patches, 128), jnp.float32),
            pltpu.VMEM((patches + EXTRA, count * width), jnp.bfloat16),
        ],
        compiler_params=pltpu.CompilerParams(vmem_limit_bytes=20 << 20),
        name="attention_block",
    )(rows, gain, *blocks, *carried, qk_gain)


def projection_block(places, order_ref, own_ref, other_ref, w_own_ref, w_other_ref, *out_refs):
    width = out_refs[0].shape[1]
    for at, out_ref in zip(places, out_refs):
        in_own = pl.ds(pl.multiple_of((order_ref[0] + order_ref[1 + at]) * width, width), width)
        in_other = pl.ds(pl.multiple_of(order_ref[1 + at] * width, width), width)
        out = jnp.dot(own_ref[...], w_own_ref[:, in_own], preferred_element_type=jnp.float32)
        out += jnp.dot(other_ref[...], w_other_ref[:, in_other], preferred_element_type=jnp.float32)
        out_ref[...] = out.astype(out_ref.dtype)


def projection(order, own, other, w_own, w_other, ring, places):
    shape = (own.shape[0], w_other.shape[1] // ring)
    out = pl.pallas_call(
        functools.partial(projection_block, places),
        out_shape=[jax.ShapeDtypeStruct(shape, jnp.bfloat16)] * len(places),
        in_specs=[SMEM] + [VMEM] * 4,
        out_specs=[VMEM] * len(places),
        compiler_params=pltpu.CompilerParams(vmem_limit_bytes=24 << 20),
        name="projection_block",
    )(order, own, other, w_own, w_other)
    return dict(zip(places, out))


def shifted(block, axis, by):
    peers = lax.axis_size(axis)
    return lax.ppermute(block, axis, [(i, (i + by) % peers) for i in range(peers)])


def across(block, by):
    ring = lax.axis_size(RING)
    pairs = [(y * ring + z, (1 - y) * ring + (z + by) % ring) for y in range(2) for z in range(ring)]
    return lax.ppermute(block, (PAIR, RING), pairs)


def to_next_section(block, by):
    sections, ring = lax.axis_size(SECTION), lax.axis_size(RING)

    def place(s, y, z):
        return ((s % sections) * 2 + y) * ring + z % ring

    pairs = [
        (place(s, y, z), place(s + 1, y, z + by)) for s in range(sections) for y in range(2) for z in range(ring)
    ]
    return lax.ppermute(block, SECTION + (PAIR, RING), pairs)


def added(*blocks):
    return functools.reduce(jnp.add, (b.astype(jnp.float32) for b in blocks)).astype(jnp.bfloat16)


def on_device(state, ln_gain, w_qkv, qk_gain, w_out):
    ring = lax.axis_size(RING)
    assert ring == 8
    here, side = lax.axis_index(RING), lax.axis_index(PAIR)
    own = state[0]
    width = own.shape[1]
    w_planes = pltpu.with_memory_space_constraint(jnp.transpose(w_qkv[0], (1, 0, 2)), pltpu.HBM)
    gain = ln_gain[0].reshape(2 * ring, 1, width)
    w_own = w_out[0]

    def rows(*places):
        return jnp.stack([(side ^ y) * ring + (here + o) % ring for y, o in places]).astype(jnp.int32)

    early_rows = rows(
        (0, 0), (1, 0), (0, -1), (0, 1), (0, -2), (0, 2), (1, -1), (1, 1), (0, -3), (0, 3), (1, -2), (1, 2)
    )
    late_rows = rows((0, -4), (1, -3), (1, 3), (1, 4))
    order = jnp.concatenate([side[None] * ring, (here + jnp.arange(ring)) % ring]).astype(jnp.int32)

    half = w_own.shape[1] // 2

    def step(_, own):
        a_up, a_down = shifted(own, RING, 1), shifted(own, RING, -1)
        other = shifted(own, PAIR, 1)
        a_up, a_down, other = lax.optimization_barrier((a_up, a_down, other))
        w_give = lax.dynamic_slice_in_dim(lax.optimization_barrier((w_own, own))[0], (1 - side) * half, half, 1)
        w_other = shifted(lax.optimization_barrier((w_give, other))[0], PAIR, 1)
        blocks = [own, other, a_up, a_down]
        b_up = b_down = other
        for _ in range(2):
            a_up, a_down = shifted(a_up, RING, 1), shifted(a_down, RING, -1)
            b_up, b_down = shifted(b_up, RING, 1), shifted(b_down, RING, -1)
            blocks += [a_up, a_down, b_up, b_down]
        late = [shifted(a_up, RING, 1), shifted(b_up, RING, 1), shifted(b_down, RING, -1), across(a_down, -1)]

        sums = partial(early_rows, late_rows, gain, w_planes, blocks)
        mixed = attention(late_rows, gain, late, sums, qk_gain[0], 2 * ring)
        mixed_other = shifted(mixed, PAIR, 1)
        parts = projection(order, mixed, mixed_other, w_own, w_other, ring, (4, 5))
        up, down = shifted(parts[4], RING, 1), shifted(parts[5], RING, -1)
        parts |= projection(order, mixed, mixed_other, w_own, w_other, ring, (3, 6, 0, 7, 2, 1))

        kept = to_next_section(added(own, parts[0]), 0)
        down = to_next_section(added(shifted(added(down, parts[6]), RING, -1), parts[7]), -1)
        for k in (3, 2):
            up = shifted(added(up, parts[k]), RING, 1)
        up = to_next_section(added(up, parts[1]), 1)
        return added(kept, down, up)

    return lax.fori_loop(0, STEPS, step, own)[None]


def solution(mesh):
    assert dict(mesh.shape) == {"section": 16, "tensor": 16}
    devices = mesh.devices.reshape(2, 4, 2, 2, 8)
    fine = Mesh(devices, SECTION + (PAIR, RING))
    tensor = (PAIR, RING)
    return jax.shard_map(
        on_device,
        mesh=fine,
        in_specs=(
            P(SECTION, None, tensor),
            P(SECTION, None),
            P(SECTION, None, None, tensor),
            P(SECTION, None, None),
            P(SECTION, tensor, None),
        ),
        out_specs=P(SECTION, None, tensor),
        check_vma=False,
    )
```

```python
import functools

import jax
import jax.numpy as jnp
from jax import lax
from jax.experimental import pallas as pl
from jax.experimental.pallas import tpu as pltpu
from jax.sharding import Mesh, PartitionSpec as P

HD = 128
STEPS = 2
EPS = 1e-06
SECTION = ("yh", "x", "core")
PAIR = "yl"
RING = "z"
EXTRA = 16
VMEM = pl.BlockSpec(memory_space=pltpu.VMEM)
SMEM = pl.BlockSpec(memory_space=pltpu.SMEM)
ROWS = 64
GROUP = 4
LATE = 4


def fetches(rows_ref, w_hbm, w_ref, w_sem, count, width):
    def fetch(at):
        start = pl.multiple_of(rows_ref[at] * width, width)
        return pltpu.make_async_copy(
            w_hbm.at[:, pl.ds(start, width), :], w_ref.at[:, pl.ds(at * width, width), :], w_sem.at[at]
        )

    return [fetch(at) for at in range(count)]


def scale_blocks(first, rows_ref, gain_ref, x_refs, before_ref, sums_ref, shift_ref, scaled_ref):
    patches, width = x_refs[0].shape
    for at in range(len(x_refs)):
        gain = gain_ref[rows_ref[at]]
        high = gain.astype(jnp.bfloat16).astype(jnp.float32)
        row = lax.broadcasted_iota(jnp.int32, (EXTRA, width), 0)
        both = jnp.where(row == 0, high, jnp.where(row == 1, gain - high, 0.0))
        scaled_ref[patches : patches + EXTRA, at * width : (at + 1) * width] = both.astype(jnp.bfloat16)

    @pl.loop(0, patches // ROWS)
    def _(block):
        part = pl.ds(pl.multiple_of(block * ROWS, ROWS), ROWS)
        if first:
            shift = jnp.sum(x_refs[0][part, :].astype(jnp.float32), axis=-1, keepdims=True) / width
            shift_ref[part, :] = jnp.broadcast_to(shift, (ROWS, 128))
            total = squares = jnp.zeros((ROWS, 128), jnp.float32)
        else:
            shift = shift_ref[part, 0:1]
            total, squares = before_ref[0, part, :], before_ref[1, part, :]
        for at, x_ref in enumerate(x_refs):
            values = x_ref[part, :].astype(jnp.float32)
            for lane in range(0, width, 128):
                piece = values[:, lane : lane + 128]
                total += piece
                squares += piece * piece
            scaled = (values - shift) * gain_ref[rows_ref[at]]
            scaled_ref[part, at * width : (at + 1) * width] = scaled.astype(jnp.bfloat16)
        sums_ref[0, part, :] = total
        sums_ref[1, part, :] = squares


def partial_block(blocks, rows_ref, late_rows_ref, gain_ref, w_hbm, *refs):
    x_refs, (acc_ref, sums_ref, shift_ref, w_late_ref, scaled_ref, w_ref, w_sem, late_sem) = refs[:blocks], refs[blocks:]
    width = x_refs[0].shape[1]
    now = fetches(rows_ref, w_hbm, w_ref, w_sem, blocks, width)
    late = fetches(late_rows_ref, w_hbm, w_late_ref, late_sem, LATE, width)
    for copy in now + late:
        copy.start()
    scale_blocks(True, rows_ref, gain_ref, x_refs, None, sums_ref, shift_ref, scaled_ref)
    for copy in now:
        copy.wait()
    depth = GROUP * width

    @pl.loop(0, 3)
    def _(plane):
        for group in range(blocks // GROUP):
            span = slice(group * depth, (group + 1) * depth)
            out = jnp.dot(scaled_ref[:, span], w_ref[plane, span, :], preferred_element_type=jnp.float32)
            if group == 0:
                acc_ref[plane] = out
            else:
                acc_ref[plane] += out

    for copy in late:
        copy.wait()


def final_block(blocks, pieces, rows_ref, gain_ref, *refs):
    x_refs, (acc_ref, before_ref, shift_ref, w_ref, qk_gain_ref, out_ref, sums_ref, scaled_ref) = (
        refs[:blocks],
        refs[blocks:],
    )
    patches, width = x_refs[0].shape
    full_width = pieces * width
    scale_blocks(False, rows_ref, gain_ref, x_refs, before_ref, sums_ref, shift_ref, scaled_ref)
    mean = jnp.sum(sums_ref[0], axis=-1, keepdims=True) / full_width
    spread = jnp.sum(sums_ref[1], axis=-1, keepdims=True) / full_width - mean * mean
    scale = lax.rsqrt(spread + EPS)
    offset = mean - shift_ref[:, 0:1]

    def projected(plane):
        out = acc_ref[plane] + jnp.dot(scaled_ref[...], w_ref[plane], preferred_element_type=jnp.float32)
        weighed = out[patches : patches + 1] + out[patches + 1 : patches + 2]
        return (out[:patches] - offset * weighed) * scale

    def head_norm(values, gain):
        mean = jnp.mean(values, axis=-1, keepdims=True)
        squares = jnp.mean(values * values, axis=-1, keepdims=True)
        return ((values - mean) * lax.rsqrt(squares - mean * mean + EPS) * gain).astype(jnp.bfloat16)

    all_query, all_keys, all_value = (projected(plane) for plane in range(3))
    for head in range(out_ref.shape[1] // HD):
        cols = slice(head * HD, (head + 1) * HD)
        query = head_norm(all_query[:, cols], qk_gain_ref[0:1, :])
        keys = head_norm(all_keys[:, cols], qk_gain_ref[1:2, :])
        value = all_value[:, cols].astype(jnp.bfloat16)
        scores = lax.dot_general(query, keys, (((1,), (1,)), ((), ())), preferred_element_type=jnp.float32)
        expo = jnp.exp(scores * HD**-0.5)
        attend = (expo * (1.0 / jnp.sum(expo, axis=-1, keepdims=True))).astype(jnp.bfloat16)
        out_ref[:, cols] = jnp.dot(attend, value, preferred_element_type=jnp.float32).astype(jnp.bfloat16)


def partial(rows, late_rows, gain, w_planes, blocks):
    patches, width = blocks[0].shape
    planes, _, cols = w_planes.shape
    count = len(blocks)
    return pl.pallas_call(
        functools.partial(partial_block, count),
        out_shape=[
            jax.ShapeDtypeStruct((planes, patches + EXTRA, cols), jnp.float32),
            jax.ShapeDtypeStruct((2, patches, 128), jnp.float32),
            jax.ShapeDtypeStruct((patches, 128), jnp.float32),
            jax.ShapeDtypeStruct((planes, LATE * width, cols), jnp.bfloat16),
        ],
        in_specs=[SMEM, SMEM, VMEM, pl.BlockSpec(memory_space=pltpu.HBM)] + [VMEM] * count,
        out_specs=[VMEM] * 4,
        scratch_shapes=[
            pltpu.VMEM((patches + EXTRA, count * width), jnp.bfloat16),
            pltpu.VMEM((planes, count * width, cols), jnp.bfloat16),
            pltpu.SemaphoreType.DMA((count,)),
            pltpu.SemaphoreType.DMA((LATE,)),
        ],
        compiler_params=pltpu.CompilerParams(vmem_limit_bytes=28 << 20),
        name="qkv_partial",
    )(rows, late_rows, gain, w_planes, *blocks)


def attention(rows, gain, blocks, carried, qk_gain, pieces):
    patches, width = blocks[0].shape
    cols = carried[0].shape[2]
    count = len(blocks)
    return pl.pallas_call(
        functools.partial(final_block, count, pieces),
        out_shape=jax.ShapeDtypeStruct((patches, cols), jnp.bfloat16),
        in_specs=[SMEM] + [VMEM] * (count + 6),
        out_specs=VMEM,
        scratch_shapes=[
            pltpu.VMEM((2, patches, 128), jnp.float32),
            pltpu.VMEM((patches + EXTRA, count * width), jnp.bfloat16),
        ],
        compiler_params=pltpu.CompilerParams(vmem_limit_bytes=20 << 20),
        name="attention_block",
    )(rows, gain, *blocks, *carried, qk_gain)


def projection_block(places, order_ref, own_ref, other_ref, w_own_ref, w_other_ref, *out_refs):
    width = out_refs[0].shape[1]
    for at, out_ref in zip(places, out_refs):
        in_own = pl.ds(pl.multiple_of((order_ref[0] + order_ref[1 + at]) * width, width), width)
        in_other = pl.ds(pl.multiple_of(order_ref[1 + at] * width, width), width)
        out = jnp.dot(own_ref[...], w_own_ref[:, in_own], preferred_element_type=jnp.float32)
        out += jnp.dot(other_ref[...], w_other_ref[:, in_other], preferred_element_type=jnp.float32)
        out_ref[...] = out.astype(out_ref.dtype)


def projection(order, own, other, w_own, w_other, ring, places):
    shape = (own.shape[0], w_other.shape[1] // ring)
    out = pl.pallas_call(
        functools.partial(projection_block, places),
        out_shape=[jax.ShapeDtypeStruct(shape, jnp.bfloat16)] * len(places),
        in_specs=[SMEM] + [VMEM] * 4,
        out_specs=[VMEM] * len(places),
        compiler_params=pltpu.CompilerParams(vmem_limit_bytes=24 << 20),
        name="projection_block",
    )(order, own, other, w_own, w_other)
    return dict(zip(places, out))


def shifted(block, axis, by):
    peers = lax.axis_size(axis)
    return lax.ppermute(block, axis, [(i, (i + by) % peers) for i in range(peers)])


def across(block, by):
    ring = lax.axis_size(RING)
    pairs = [(y * ring + z, (1 - y) * ring + (z + by) % ring) for y in range(2) for z in range(ring)]
    return lax.ppermute(block, (PAIR, RING), pairs)


def turns(section):
    return section % 8 == 7


def to_next_section(block, by):
    sections, ring = lax.axis_size(SECTION), lax.axis_size(RING)

    def place(s, y, z):
        return ((s % sections) * 2 + y) * ring + z % ring

    pairs = [
        (place(s, y, z), place(s + 1, 1 - y if turns(s) else y, z + by))
        for s in range(sections)
        for y in range(2)
        for z in range(ring)
    ]
    return lax.ppermute(block, SECTION + (PAIR, RING), pairs)


def added(*blocks):
    return functools.reduce(jnp.add, (b.astype(jnp.float32) for b in blocks)).astype(jnp.bfloat16)


def on_device(state, ln_gain, w_qkv, qk_gain, w_out):
    ring = lax.axis_size(RING)
    assert ring == 8
    here, side = lax.axis_index(RING), lax.axis_index(PAIR)
    own = state[0]
    width = own.shape[1]
    flip = turns(lax.axis_index(SECTION))
    kept_side = side ^ flip.astype(side.dtype)
    w_planes = pltpu.with_memory_space_constraint(jnp.transpose(w_qkv[0], (1, 0, 2)), pltpu.HBM)
    gain = ln_gain[0].reshape(2 * ring, 1, width)
    w_own = w_out[0]

    def rows(*places):
        return jnp.stack([(side ^ y) * ring + (here + o) % ring for y, o in places]).astype(jnp.int32)

    early_rows = rows(
        (0, 0), (1, 0), (0, -1), (0, 1), (0, -2), (0, 2), (1, -1), (1, 1), (0, -3), (0, 3), (1, -2), (1, 2)
    )
    late_rows = rows((0, -4), (1, -3), (1, 3), (1, 4))
    order = jnp.concatenate([kept_side[None] * ring, (here + jnp.arange(ring)) % ring]).astype(jnp.int32)

    half = w_own.shape[1] // 2

    def step(_, own):
        a_up, a_down = shifted(own, RING, 1), shifted(own, RING, -1)
        other = shifted(own, PAIR, 1)
        a_up, a_down, other = lax.optimization_barrier((a_up, a_down, other))
        w_give = lax.dynamic_slice_in_dim(lax.optimization_barrier((w_own, own))[0], (1 - kept_side) * half, half, 1)
        w_other = shifted(lax.optimization_barrier((w_give, other))[0], PAIR, 1)
        blocks = [own, other, a_up, a_down]
        b_up = b_down = other
        for _ in range(2):
            a_up, a_down = shifted(a_up, RING, 1), shifted(a_down, RING, -1)
            b_up, b_down = shifted(b_up, RING, 1), shifted(b_down, RING, -1)
            blocks += [a_up, a_down, b_up, b_down]
        late = [shifted(a_up, RING, 1), shifted(b_up, RING, 1), shifted(b_down, RING, -1), across(a_down, -1)]

        sums = partial(early_rows, late_rows, gain, w_planes, blocks)
        mixed = attention(late_rows, gain, late, sums, qk_gain[0], 2 * ring)
        mixed_other = shifted(mixed, PAIR, 1)
        parts = projection(order, mixed, mixed_other, w_own, w_other, ring, (4,))
        up = shifted(parts[4], RING, 1)
        mixed_other = lax.optimization_barrier((mixed_other, parts[4]))[0]
        parts |= projection(order, mixed, mixed_other, w_own, w_other, ring, (5, 3, 6, 0, 7, 2, 1))
        down = shifted(parts[5], RING, -1)

        kept = to_next_section(added(jnp.where(flip, other, own), parts[0]), 0)
        down = to_next_section(added(shifted(added(down, parts[6]), RING, -1), parts[7]), -1)
        for k in (3, 2):
            up = shifted(added(up, parts[k]), RING, 1)
        up = to_next_section(added(up, parts[1]), 1)
        return added(kept, down, up)

    return lax.fori_loop(0, STEPS, step, own)[None]


def solution(mesh):
    assert dict(mesh.shape) == {"section": 16, "tensor": 16}
    devices = mesh.devices.reshape(2, 4, 2, 2, 8)
    fine = Mesh(devices, SECTION + (PAIR, RING))
    tensor = (PAIR, RING)
    return jax.shard_map(
        on_device,
        mesh=fine,
        in_specs=(
            P(SECTION, None, tensor),
            P(SECTION, None),
            P(SECTION, None, None, tensor),
            P(SECTION, None, None),
            P(SECTION, tensor, None),
        ),
        out_specs=P(SECTION, None, tensor),
        check_vma=False,
    )
```

```python
import functools

import jax
import jax.numpy as jnp
from jax import lax
from jax.experimental import pallas as pl
from jax.experimental.pallas import tpu as pltpu
from jax.sharding import Mesh, PartitionSpec as P

HD = 128
STEPS = 2
EPS = 1e-06
SECTION = ("yh", "x", "core")
PAIR = "yl"
RING = "z"
EXTRA = 16
VMEM = pl.BlockSpec(memory_space=pltpu.VMEM)
SMEM = pl.BlockSpec(memory_space=pltpu.SMEM)
ROWS = 64
GROUP = 4
LATE = 4


def fetches(rows_ref, w_hbm, w_ref, w_sem, count, width):
    def fetch(at):
        start = pl.multiple_of(rows_ref[at] * width, width)
        return pltpu.make_async_copy(
            w_hbm.at[:, pl.ds(start, width), :], w_ref.at[:, pl.ds(at * width, width), :], w_sem.at[at]
        )

    return [fetch(at) for at in range(count)]


def scale_blocks(first, rows_ref, gain_ref, x_refs, before_ref, sums_ref, shift_ref, scaled_ref):
    patches, width = x_refs[0].shape
    for at in range(len(x_refs)):
        gain = gain_ref[rows_ref[at]]
        high = gain.astype(jnp.bfloat16).astype(jnp.float32)
        row = lax.broadcasted_iota(jnp.int32, (EXTRA, width), 0)
        both = jnp.where(row == 0, high, jnp.where(row == 1, gain - high, 0.0))
        scaled_ref[patches : patches + EXTRA, at * width : (at + 1) * width] = both.astype(jnp.bfloat16)

    @pl.loop(0, patches // ROWS)
    def _(block):
        part = pl.ds(pl.multiple_of(block * ROWS, ROWS), ROWS)
        if first:
            shift = jnp.sum(x_refs[0][part, :].astype(jnp.float32), axis=-1, keepdims=True) / width
            shift_ref[part, :] = jnp.broadcast_to(shift, (ROWS, 128))
            total = squares = jnp.zeros((ROWS, 128), jnp.float32)
        else:
            shift = shift_ref[part, 0:1]
            total, squares = before_ref[0, part, :], before_ref[1, part, :]
        for at, x_ref in enumerate(x_refs):
            values = x_ref[part, :].astype(jnp.float32)
            for lane in range(0, width, 128):
                piece = values[:, lane : lane + 128]
                total += piece
                squares += piece * piece
            scaled = (values - shift) * gain_ref[rows_ref[at]]
            scaled_ref[part, at * width : (at + 1) * width] = scaled.astype(jnp.bfloat16)
        sums_ref[0, part, :] = total
        sums_ref[1, part, :] = squares


def partial_block(blocks, rows_ref, late_rows_ref, gain_ref, w_hbm, *refs):
    x_refs, (acc_ref, sums_ref, shift_ref, w_late_ref, scaled_ref, w_ref, w_sem, late_sem) = refs[:blocks], refs[blocks:]
    width = x_refs[0].shape[1]
    now = fetches(rows_ref, w_hbm, w_ref, w_sem, blocks, width)
    late = fetches(late_rows_ref, w_hbm, w_late_ref, late_sem, LATE, width)
    for copy in now + late:
        copy.start()
    scale_blocks(True, rows_ref, gain_ref, x_refs, None, sums_ref, shift_ref, scaled_ref)
    for copy in now:
        copy.wait()
    depth = GROUP * width

    @pl.loop(0, 3)
    def _(plane):
        for group in range(blocks // GROUP):
            span = slice(group * depth, (group + 1) * depth)
            out = jnp.dot(scaled_ref[:, span], w_ref[plane, span, :], preferred_element_type=jnp.float32)
            if group == 0:
                acc_ref[plane] = out
            else:
                acc_ref[plane] += out

    for copy in late:
        copy.wait()


def final_block(blocks, pieces, rows_ref, gain_ref, *refs):
    x_refs, (acc_ref, before_ref, shift_ref, w_ref, qk_gain_ref, out_ref, sums_ref, scaled_ref) = (
        refs[:blocks],
        refs[blocks:],
    )
    patches, width = x_refs[0].shape
    full_width = pieces * width
    scale_blocks(False, rows_ref, gain_ref, x_refs, before_ref, sums_ref, shift_ref, scaled_ref)
    mean = jnp.sum(sums_ref[0], axis=-1, keepdims=True) / full_width
    spread = jnp.sum(sums_ref[1], axis=-1, keepdims=True) / full_width - mean * mean
    scale = lax.rsqrt(spread + EPS)
    offset = mean - shift_ref[:, 0:1]

    def projected(plane):
        out = acc_ref[plane] + jnp.dot(scaled_ref[...], w_ref[plane], preferred_element_type=jnp.float32)
        weighed = out[patches : patches + 1] + out[patches + 1 : patches + 2]
        return (out[:patches] - offset * weighed) * scale

    def head_norm(values, gain):
        mean = jnp.mean(values, axis=-1, keepdims=True)
        squares = jnp.mean(values * values, axis=-1, keepdims=True)
        return ((values - mean) * lax.rsqrt(squares - mean * mean + EPS) * gain).astype(jnp.bfloat16)

    all_query, all_keys, all_value = (projected(plane) for plane in range(3))
    for head in range(out_ref.shape[1] // HD):
        cols = slice(head * HD, (head + 1) * HD)
        query = head_norm(all_query[:, cols], qk_gain_ref[0:1, :])
        keys = head_norm(all_keys[:, cols], qk_gain_ref[1:2, :])
        value = all_value[:, cols].astype(jnp.bfloat16)
        scores = lax.dot_general(query, keys, (((1,), (1,)), ((), ())), preferred_element_type=jnp.float32)
        expo = jnp.exp(scores * HD**-0.5)
        attend = (expo * (1.0 / jnp.sum(expo, axis=-1, keepdims=True))).astype(jnp.bfloat16)
        out_ref[:, cols] = jnp.dot(attend, value, preferred_element_type=jnp.float32).astype(jnp.bfloat16)


def partial(rows, late_rows, gain, w_planes, blocks):
    patches, width = blocks[0].shape
    planes, _, cols = w_planes.shape
    count = len(blocks)
    return pl.pallas_call(
        functools.partial(partial_block, count),
        out_shape=[
            jax.ShapeDtypeStruct((planes, patches + EXTRA, cols), jnp.float32),
            jax.ShapeDtypeStruct((2, patches, 128), jnp.float32),
            jax.ShapeDtypeStruct((patches, 128), jnp.float32),
            jax.ShapeDtypeStruct((planes, LATE * width, cols), jnp.bfloat16),
        ],
        in_specs=[SMEM, SMEM, VMEM, pl.BlockSpec(memory_space=pltpu.HBM)] + [VMEM] * count,
        out_specs=[VMEM] * 4,
        scratch_shapes=[
            pltpu.VMEM((patches + EXTRA, count * width), jnp.bfloat16),
            pltpu.VMEM((planes, count * width, cols), jnp.bfloat16),
            pltpu.SemaphoreType.DMA((count,)),
            pltpu.SemaphoreType.DMA((LATE,)),
        ],
        compiler_params=pltpu.CompilerParams(vmem_limit_bytes=28 << 20),
        name="qkv_partial",
    )(rows, late_rows, gain, w_planes, *blocks)


def attention(rows, gain, blocks, carried, qk_gain, pieces):
    patches, width = blocks[0].shape
    cols = carried[0].shape[2]
    count = len(blocks)
    return pl.pallas_call(
        functools.partial(final_block, count, pieces),
        out_shape=jax.ShapeDtypeStruct((patches, cols), jnp.bfloat16),
        in_specs=[SMEM] + [VMEM] * (count + 6),
        out_specs=VMEM,
        scratch_shapes=[
            pltpu.VMEM((2, patches, 128), jnp.float32),
            pltpu.VMEM((patches + EXTRA, count * width), jnp.bfloat16),
        ],
        compiler_params=pltpu.CompilerParams(vmem_limit_bytes=20 << 20),
        name="attention_block",
    )(rows, gain, *blocks, *carried, qk_gain)


def projection_block(places, order_ref, own_ref, other_ref, w_own_ref, w_other_ref, *out_refs):
    width = out_refs[0].shape[1]
    for at, out_ref in zip(places, out_refs):
        in_own = pl.ds(pl.multiple_of((order_ref[0] + order_ref[1 + at]) * width, width), width)
        in_other = pl.ds(pl.multiple_of(order_ref[1 + at] * width, width), width)
        out = jnp.dot(own_ref[...], w_own_ref[:, in_own], preferred_element_type=jnp.float32)
        out += jnp.dot(other_ref[...], w_other_ref[:, in_other], preferred_element_type=jnp.float32)
        out_ref[...] = out.astype(out_ref.dtype)


def projection(order, own, other, w_own, w_other, ring, places):
    shape = (own.shape[0], w_other.shape[1] // ring)
    out = pl.pallas_call(
        functools.partial(projection_block, places),
        out_shape=[jax.ShapeDtypeStruct(shape, jnp.bfloat16)] * len(places),
        in_specs=[SMEM] + [VMEM] * 4,
        out_specs=[VMEM] * len(places),
        compiler_params=pltpu.CompilerParams(vmem_limit_bytes=24 << 20),
        name="projection_block",
    )(order, own, other, w_own, w_other)
    return dict(zip(places, out))


def shifted(block, axis, by):
    peers = lax.axis_size(axis)
    return lax.ppermute(block, axis, [(i, (i + by) % peers) for i in range(peers)])


def across(block, by):
    ring = lax.axis_size(RING)
    pairs = [(y * ring + z, (1 - y) * ring + (z + by) % ring) for y in range(2) for z in range(ring)]
    return lax.ppermute(block, (PAIR, RING), pairs)


def turns(section):
    return section % 8 == 7


def to_next_section(block, by):
    sections, ring = lax.axis_size(SECTION), lax.axis_size(RING)

    def place(s, y, z):
        return ((s % sections) * 2 + y) * ring + z % ring

    pairs = [
        (place(s, y, z), place(s + 1, 1 - y if turns(s) else y, z + by))
        for s in range(sections)
        for y in range(2)
        for z in range(ring)
    ]
    return lax.ppermute(block, SECTION + (PAIR, RING), pairs)


def added(*blocks):
    return functools.reduce(jnp.add, (b.astype(jnp.float32) for b in blocks)).astype(jnp.bfloat16)


def on_device(state, ln_gain, w_qkv, qk_gain, w_out):
    ring = lax.axis_size(RING)
    assert ring == 8
    here, side = lax.axis_index(RING), lax.axis_index(PAIR)
    own = state[0]
    width = own.shape[1]
    flip = turns(lax.axis_index(SECTION))
    kept_side = side ^ flip.astype(side.dtype)
    w_planes = pltpu.with_memory_space_constraint(jnp.transpose(w_qkv[0], (1, 0, 2)), pltpu.HBM)
    gain = ln_gain[0].reshape(2 * ring, 1, width)
    w_own = w_out[0]

    def rows(*places):
        return jnp.stack([(side ^ y) * ring + (here + o) % ring for y, o in places]).astype(jnp.int32)

    early_rows = rows(
        (0, 0), (1, 0), (0, -1), (0, 1), (0, -2), (0, 2), (1, -1), (1, 1), (0, -3), (0, 3), (1, -2), (1, 2)
    )
    late_rows = rows((0, -4), (1, -3), (1, 3), (1, 4))
    order = jnp.concatenate([kept_side[None] * ring, (here + jnp.arange(ring)) % ring]).astype(jnp.int32)

    half = w_own.shape[1] // 2

    def step(_, own):
        a_up, a_down = shifted(own, RING, 1), shifted(own, RING, -1)
        other = shifted(own, PAIR, 1)
        a_up, a_down = lax.optimization_barrier((a_up, a_down))
        w_give = lax.dynamic_slice_in_dim(lax.optimization_barrier((w_own, own))[0], (1 - kept_side) * half, half, 1)
        blocks = [own, other, a_up, a_down]
        b_up = b_down = other
        for _ in range(2):
            a_up, a_down = shifted(a_up, RING, 1), shifted(a_down, RING, -1)
            b_up, b_down = shifted(b_up, RING, 1), shifted(b_down, RING, -1)
            blocks += [a_up, a_down, b_up, b_down]
            if len(blocks) == 8:
                w_other = shifted(lax.optimization_barrier((w_give, a_up, a_down, b_up, b_down))[0], PAIR, 1)
        late = [shifted(a_up, RING, 1), shifted(b_up, RING, 1), shifted(b_down, RING, -1), across(a_down, -1)]

        sums = partial(early_rows, late_rows, gain, w_planes, blocks)
        mixed = attention(late_rows, gain, late, sums, qk_gain[0], 2 * ring)
        mixed_other = shifted(mixed, PAIR, 1)
        parts = projection(order, mixed, mixed_other, w_own, w_other, ring, (4,))
        up = shifted(parts[4], RING, 1)
        mixed_other = lax.optimization_barrier((mixed_other, parts[4]))[0]
        parts |= projection(order, mixed, mixed_other, w_own, w_other, ring, (5, 3, 6, 0, 7, 2, 1))
        down = shifted(parts[5], RING, -1)

        kept = to_next_section(added(jnp.where(flip, other, own), parts[0]), 0)
        down = to_next_section(added(shifted(added(down, parts[6]), RING, -1), parts[7]), -1)
        for k in (3, 2):
            up = shifted(added(up, parts[k]), RING, 1)
        up = to_next_section(added(up, parts[1]), 1)
        return added(kept, down, up)

    return lax.fori_loop(0, STEPS, step, own)[None]


def solution(mesh):
    assert dict(mesh.shape) == {"section": 16, "tensor": 16}
    devices = mesh.devices.reshape(2, 4, 2, 2, 8)
    fine = Mesh(devices, SECTION + (PAIR, RING))
    tensor = (PAIR, RING)
    return jax.shard_map(
        on_device,
        mesh=fine,
        in_specs=(
            P(SECTION, None, tensor),
            P(SECTION, None),
            P(SECTION, None, None, tensor),
            P(SECTION, None, None),
            P(SECTION, tensor, None),
        ),
        out_specs=P(SECTION, None, tensor),
        check_vma=False,
    )
```

```python
import functools

import jax
import jax.numpy as jnp
from jax import lax
from jax.experimental import pallas as pl
from jax.experimental.pallas import tpu as pltpu
from jax.sharding import Mesh, PartitionSpec as P

HD = 128
STEPS = 2
EPS = 1e-06
SECTION = ("yh", "x", "core")
PAIR = "yl"
RING = "z"
EXTRA = 16
VMEM = pl.BlockSpec(memory_space=pltpu.VMEM)
SMEM = pl.BlockSpec(memory_space=pltpu.SMEM)
ROWS = 64
GROUP = 4
LATE = 4


def fetches(rows_ref, w_hbm, w_ref, w_sem, count, width):
    def fetch(at):
        start = pl.multiple_of(rows_ref[at] * width, width)
        return pltpu.make_async_copy(
            w_hbm.at[:, pl.ds(start, width), :], w_ref.at[:, pl.ds(at * width, width), :], w_sem.at[at]
        )

    return [fetch(at) for at in range(count)]


def scale_blocks(first, rows_ref, gain_ref, x_refs, before_ref, sums_ref, shift_ref, scaled_ref):
    patches, width = x_refs[0].shape
    for at in range(len(x_refs)):
        gain = gain_ref[rows_ref[at]]
        high = gain.astype(jnp.bfloat16).astype(jnp.float32)
        row = lax.broadcasted_iota(jnp.int32, (EXTRA, width), 0)
        both = jnp.where(row == 0, high, jnp.where(row == 1, gain - high, 0.0))
        scaled_ref[patches : patches + EXTRA, at * width : (at + 1) * width] = both.astype(jnp.bfloat16)

    @pl.loop(0, patches // ROWS)
    def _(block):
        part = pl.ds(pl.multiple_of(block * ROWS, ROWS), ROWS)
        if first:
            shift = jnp.sum(x_refs[0][part, :].astype(jnp.float32), axis=-1, keepdims=True) / width
            shift_ref[part, :] = jnp.broadcast_to(shift, (ROWS, 128))
            total = squares = jnp.zeros((ROWS, 128), jnp.float32)
        else:
            shift = shift_ref[part, 0:1]
            total, squares = before_ref[0, part, :], before_ref[1, part, :]
        for at, x_ref in enumerate(x_refs):
            values = x_ref[part, :].astype(jnp.float32)
            for lane in range(0, width, 128):
                piece = values[:, lane : lane + 128]
                total += piece
                squares += piece * piece
            scaled = (values - shift) * gain_ref[rows_ref[at]]
            scaled_ref[part, at * width : (at + 1) * width] = scaled.astype(jnp.bfloat16)
        sums_ref[0, part, :] = total
        sums_ref[1, part, :] = squares


def single(refs):
    return [view for ref in refs for view in ([ref] if len(ref.shape) == 2 else [ref.at[i] for i in range(ref.shape[0])])]


def partial_block(arrays, rows_ref, late_rows_ref, gain_ref, w_hbm, *refs):
    acc_ref, sums_ref, shift_ref, w_late_ref, scaled_ref, w_ref, w_sem, late_sem = refs[arrays:]
    x_refs = single(refs[:arrays])
    blocks, width = len(x_refs), x_refs[0].shape[1]
    now = fetches(rows_ref, w_hbm, w_ref, w_sem, blocks, width)
    late = fetches(late_rows_ref, w_hbm, w_late_ref, late_sem, LATE, width)
    for copy in now + late:
        copy.start()
    scale_blocks(True, rows_ref, gain_ref, x_refs, None, sums_ref, shift_ref, scaled_ref)
    for copy in now:
        copy.wait()
    depth = GROUP * width

    @pl.loop(0, 3)
    def _(plane):
        for group in range(blocks // GROUP):
            span = slice(group * depth, (group + 1) * depth)
            out = jnp.dot(scaled_ref[:, span], w_ref[plane, span, :], preferred_element_type=jnp.float32)
            if group == 0:
                acc_ref[plane] = out
            else:
                acc_ref[plane] += out

    for copy in late:
        copy.wait()


def final_block(arrays, pieces, rows_ref, gain_ref, *refs):
    acc_ref, before_ref, shift_ref, w_ref, qk_gain_ref, out_ref, sums_ref, scaled_ref = refs[arrays:]
    x_refs = single(refs[:arrays])
    patches, width = x_refs[0].shape
    full_width = pieces * width
    scale_blocks(False, rows_ref, gain_ref, x_refs, before_ref, sums_ref, shift_ref, scaled_ref)
    mean = jnp.sum(sums_ref[0], axis=-1, keepdims=True) / full_width
    spread = jnp.sum(sums_ref[1], axis=-1, keepdims=True) / full_width - mean * mean
    scale = lax.rsqrt(spread + EPS)
    offset = mean - shift_ref[:, 0:1]

    def projected(plane):
        out = acc_ref[plane] + jnp.dot(scaled_ref[...], w_ref[plane], preferred_element_type=jnp.float32)
        weighed = out[patches : patches + 1] + out[patches + 1 : patches + 2]
        return (out[:patches] - offset * weighed) * scale

    def head_norm(values, gain):
        mean = jnp.mean(values, axis=-1, keepdims=True)
        squares = jnp.mean(values * values, axis=-1, keepdims=True)
        return ((values - mean) * lax.rsqrt(squares - mean * mean + EPS) * gain).astype(jnp.bfloat16)

    all_query, all_keys, all_value = (projected(plane) for plane in range(3))
    for head in range(out_ref.shape[1] // HD):
        cols = slice(head * HD, (head + 1) * HD)
        query = head_norm(all_query[:, cols], qk_gain_ref[0:1, :])
        keys = head_norm(all_keys[:, cols], qk_gain_ref[1:2, :])
        value = all_value[:, cols].astype(jnp.bfloat16)
        scores = lax.dot_general(query, keys, (((1,), (1,)), ((), ())), preferred_element_type=jnp.float32)
        expo = jnp.exp(scores * HD**-0.5)
        attend = (expo * (1.0 / jnp.sum(expo, axis=-1, keepdims=True))).astype(jnp.bfloat16)
        out_ref[:, cols] = jnp.dot(attend, value, preferred_element_type=jnp.float32).astype(jnp.bfloat16)


def partial(rows, late_rows, gain, w_planes, blocks):
    patches, width = blocks[0].shape
    planes, _, cols = w_planes.shape
    count = rows.shape[0]
    return pl.pallas_call(
        functools.partial(partial_block, len(blocks)),
        out_shape=[
            jax.ShapeDtypeStruct((planes, patches + EXTRA, cols), jnp.float32),
            jax.ShapeDtypeStruct((2, patches, 128), jnp.float32),
            jax.ShapeDtypeStruct((patches, 128), jnp.float32),
            jax.ShapeDtypeStruct((planes, LATE * width, cols), jnp.bfloat16),
        ],
        in_specs=[SMEM, SMEM, VMEM, pl.BlockSpec(memory_space=pltpu.HBM)] + [VMEM] * len(blocks),
        out_specs=[VMEM] * 4,
        scratch_shapes=[
            pltpu.VMEM((patches + EXTRA, count * width), jnp.bfloat16),
            pltpu.VMEM((planes, count * width, cols), jnp.bfloat16),
            pltpu.SemaphoreType.DMA((count,)),
            pltpu.SemaphoreType.DMA((LATE,)),
        ],
        compiler_params=pltpu.CompilerParams(vmem_limit_bytes=28 << 20),
        name="qkv_partial",
    )(rows, late_rows, gain, w_planes, *blocks)


def attention(rows, gain, blocks, carried, qk_gain, pieces):
    patches, width = blocks[-1].shape
    cols = carried[0].shape[2]
    count = rows.shape[0]
    return pl.pallas_call(
        functools.partial(final_block, len(blocks), pieces),
        out_shape=jax.ShapeDtypeStruct((patches, cols), jnp.bfloat16),
        in_specs=[SMEM] + [VMEM] * (len(blocks) + 6),
        out_specs=VMEM,
        scratch_shapes=[
            pltpu.VMEM((2, patches, 128), jnp.float32),
            pltpu.VMEM((patches + EXTRA, count * width), jnp.bfloat16),
        ],
        compiler_params=pltpu.CompilerParams(vmem_limit_bytes=20 << 20),
        name="attention_block",
    )(rows, gain, *blocks, *carried, qk_gain)


def projection_block(places, order_ref, own_ref, other_ref, w_own_ref, w_other_ref, *out_refs):
    width = out_refs[0].shape[1]
    for at, out_ref in zip(places, out_refs):
        in_own = pl.ds(pl.multiple_of((order_ref[0] + order_ref[1 + at]) * width, width), width)
        in_other = pl.ds(pl.multiple_of(order_ref[1 + at] * width, width), width)
        out = jnp.dot(own_ref[...], w_own_ref[:, in_own], preferred_element_type=jnp.float32)
        out += jnp.dot(other_ref[...], w_other_ref[:, in_other], preferred_element_type=jnp.float32)
        out_ref[...] = out.astype(out_ref.dtype)


def projection(order, own, other, w_own, w_other, ring, places):
    shape = (own.shape[0], w_other.shape[1] // ring)
    out = pl.pallas_call(
        functools.partial(projection_block, places),
        out_shape=[jax.ShapeDtypeStruct(shape, jnp.bfloat16)] * len(places),
        in_specs=[SMEM] + [VMEM] * 4,
        out_specs=[VMEM] * len(places),
        compiler_params=pltpu.CompilerParams(vmem_limit_bytes=24 << 20),
        name="projection_block",
    )(order, own, other, w_own, w_other)
    return dict(zip(places, out))


def shifted(block, axis, by):
    peers = lax.axis_size(axis)
    return lax.ppermute(block, axis, [(i, (i + by) % peers) for i in range(peers)])


def across(block, by):
    ring = lax.axis_size(RING)
    pairs = [(y * ring + z, (1 - y) * ring + (z + by) % ring) for y in range(2) for z in range(ring)]
    return lax.ppermute(block, (PAIR, RING), pairs)


def turns(section):
    return section % 8 == 7


def to_next_section(block, by):
    sections, ring = lax.axis_size(SECTION), lax.axis_size(RING)

    def place(s, y, z):
        return ((s % sections) * 2 + y) * ring + z % ring

    pairs = [
        (place(s, y, z), place(s + 1, 1 - y if turns(s) else y, z + by))
        for s in range(sections)
        for y in range(2)
        for z in range(ring)
    ]
    return lax.ppermute(block, SECTION + (PAIR, RING), pairs)


def added(*blocks):
    return functools.reduce(jnp.add, (b.astype(jnp.float32) for b in blocks)).astype(jnp.bfloat16)


def on_device(state, ln_gain, w_qkv, qk_gain, w_out):
    ring = lax.axis_size(RING)
    assert ring == 8
    here, side = lax.axis_index(RING), lax.axis_index(PAIR)
    own = state[0]
    width = own.shape[1]
    flip = turns(lax.axis_index(SECTION))
    kept_side = side ^ flip.astype(side.dtype)
    w_planes = pltpu.with_memory_space_constraint(jnp.transpose(w_qkv[0], (1, 0, 2)), pltpu.HBM)
    gain = ln_gain[0].reshape(2 * ring, 1, width)
    w_own = w_out[0]

    def rows(*places):
        return jnp.stack([(side ^ y) * ring + (here + o) % ring for y, o in places]).astype(jnp.int32)

    early_rows = rows(
        (0, 0), (1, 0), (0, -1), (0, 1), (0, -2), (1, -1), (0, 2), (1, 1), (0, -3), (1, -2), (0, 3), (1, 2)
    )
    late_rows = rows((0, -4), (1, -3), (1, 3), (1, 4))
    order = jnp.concatenate([kept_side[None] * ring, (here + jnp.arange(ring)) % ring]).astype(jnp.int32)

    half = w_own.shape[1] // 2

    def step(_, own):
        a_up, a_down = shifted(own, RING, 1), shifted(own, RING, -1)
        other = shifted(own, PAIR, 1)
        a_up, a_down, other = lax.optimization_barrier((a_up, a_down, other))
        w_give = lax.dynamic_slice_in_dim(lax.optimization_barrier((w_own, own))[0], (1 - kept_side) * half, half, 1)
        w_other = shifted(lax.optimization_barrier((w_give, other))[0], PAIR, 1)
        blocks = [own, other, a_up, a_down]
        up, down = jnp.stack([a_up, other]), jnp.stack([a_down, other])
        for _ in range(2):
            up, down = shifted(up, RING, 1), shifted(down, RING, -1)
            blocks += [up, down]
        late = [shifted(up, RING, 1), shifted(down[1], RING, -1), across(down[0], -1)]

        sums = partial(early_rows, late_rows, gain, w_planes, blocks)
        mixed = attention(late_rows, gain, late, sums, qk_gain[0], 2 * ring)
        mixed_other = shifted(mixed, PAIR, 1)
        parts = projection(order, mixed, mixed_other, w_own, w_other, ring, (4,))
        up = shifted(parts[4], RING, 1)
        mixed_other = lax.optimization_barrier((mixed_other, parts[4]))[0]
        parts |= projection(order, mixed, mixed_other, w_own, w_other, ring, (5, 3, 6, 0, 7, 2, 1))
        down = shifted(parts[5], RING, -1)

        kept = to_next_section(added(jnp.where(flip, other, own), parts[0]), 0)
        down = to_next_section(added(shifted(added(down, parts[6]), RING, -1), parts[7]), -1)
        for k in (3, 2):
            up = shifted(added(up, parts[k]), RING, 1)
        up = to_next_section(added(up, parts[1]), 1)
        return added(kept, down, up)

    return lax.fori_loop(0, STEPS, step, own)[None]


def solution(mesh):
    assert dict(mesh.shape) == {"section": 16, "tensor": 16}
    devices = mesh.devices.reshape(2, 4, 2, 2, 8)
    fine = Mesh(devices, SECTION + (PAIR, RING))
    tensor = (PAIR, RING)
    return jax.shard_map(
        on_device,
        mesh=fine,
        in_specs=(
            P(SECTION, None, tensor),
            P(SECTION, None),
            P(SECTION, None, None, tensor),
            P(SECTION, None, None),
            P(SECTION, tensor, None),
        ),
        out_specs=P(SECTION, None, tensor),
        check_vma=False,
    )
```

```python
import functools

import jax
import jax.numpy as jnp
from jax import lax
from jax.experimental import pallas as pl
from jax.experimental.pallas import tpu as pltpu
from jax.sharding import Mesh, PartitionSpec as P

HD = 128
STEPS = 2
EPS = 1e-06
SECTION = ("yh", "x", "core")
PAIR = "yl"
RING = "z"
EXTRA = 16
VMEM = pl.BlockSpec(memory_space=pltpu.VMEM)
SMEM = pl.BlockSpec(memory_space=pltpu.SMEM)
ROWS = 64
GROUP = 2
LATE = 2


def fetches(rows_ref, w_hbm, w_ref, w_sem, count, width):
    def fetch(at):
        start = pl.multiple_of(rows_ref[at] * width, width)
        return pltpu.make_async_copy(
            w_hbm.at[:, pl.ds(start, width), :], w_ref.at[:, pl.ds(at * width, width), :], w_sem.at[at]
        )

    return [fetch(at) for at in range(count)]


def scale_blocks(first, rows_ref, gain_ref, x_refs, before_ref, sums_ref, shift_ref, scaled_ref):
    patches, width = x_refs[0].shape
    for at in range(len(x_refs)):
        gain = gain_ref[rows_ref[at]]
        high = gain.astype(jnp.bfloat16).astype(jnp.float32)
        row = lax.broadcasted_iota(jnp.int32, (EXTRA, width), 0)
        both = jnp.where(row == 0, high, jnp.where(row == 1, gain - high, 0.0))
        scaled_ref[patches : patches + EXTRA, at * width : (at + 1) * width] = both.astype(jnp.bfloat16)

    @pl.loop(0, patches // ROWS)
    def _(block):
        part = pl.ds(pl.multiple_of(block * ROWS, ROWS), ROWS)
        if first:
            shift = jnp.sum(x_refs[0][part, :].astype(jnp.float32), axis=-1, keepdims=True) / width
            shift_ref[part, :] = jnp.broadcast_to(shift, (ROWS, 128))
            total = squares = jnp.zeros((ROWS, 128), jnp.float32)
        else:
            shift = shift_ref[part, 0:1]
            total, squares = before_ref[0, part, :], before_ref[1, part, :]
        for at, x_ref in enumerate(x_refs):
            values = x_ref[part, :].astype(jnp.float32)
            for lane in range(0, width, 128):
                piece = values[:, lane : lane + 128]
                total += piece
                squares += piece * piece
            scaled = (values - shift) * gain_ref[rows_ref[at]]
            scaled_ref[part, at * width : (at + 1) * width] = scaled.astype(jnp.bfloat16)
        sums_ref[0, part, :] = total
        sums_ref[1, part, :] = squares


def partial_block(blocks, rows_ref, late_rows_ref, gain_ref, w_hbm, *refs):
    x_refs, (acc_ref, sums_ref, shift_ref, w_late_ref, scaled_ref, w_ref, w_sem, late_sem) = refs[:blocks], refs[blocks:]
    width = x_refs[0].shape[1]
    now = fetches(rows_ref, w_hbm, w_ref, w_sem, blocks, width)
    late = fetches(late_rows_ref, w_hbm, w_late_ref, late_sem, LATE, width)
    for copy in now + late:
        copy.start()
    scale_blocks(True, rows_ref, gain_ref, x_refs, None, sums_ref, shift_ref, scaled_ref)
    for copy in now:
        copy.wait()
    depth = GROUP * width

    @pl.loop(0, 3)
    def _(plane):
        for group in range(blocks // GROUP):
            span = slice(group * depth, (group + 1) * depth)
            out = jnp.dot(scaled_ref[:, span], w_ref[plane, span, :], preferred_element_type=jnp.float32)
            if group == 0:
                acc_ref[plane] = out
            else:
                acc_ref[plane] += out

    for copy in late:
        copy.wait()


def final_block(blocks, pieces, rows_ref, gain_ref, *refs):
    x_refs, (acc_ref, before_ref, shift_ref, w_ref, qk_gain_ref, out_ref, sums_ref, scaled_ref) = (
        refs[:blocks],
        refs[blocks:],
    )
    patches, width = x_refs[0].shape
    full_width = pieces * width
    scale_blocks(False, rows_ref, gain_ref, x_refs, before_ref, sums_ref, shift_ref, scaled_ref)
    mean = jnp.sum(sums_ref[0], axis=-1, keepdims=True) / full_width
    spread = jnp.sum(sums_ref[1], axis=-1, keepdims=True) / full_width - mean * mean
    scale = lax.rsqrt(spread + EPS)
    offset = mean - shift_ref[:, 0:1]

    def projected(plane):
        out = acc_ref[plane] + jnp.dot(scaled_ref[...], w_ref[plane], preferred_element_type=jnp.float32)
        weighed = out[patches : patches + 1] + out[patches + 1 : patches + 2]
        return (out[:patches] - offset * weighed) * scale

    def head_norm(values, gain):
        mean = jnp.mean(values, axis=-1, keepdims=True)
        squares = jnp.mean(values * values, axis=-1, keepdims=True)
        return ((values - mean) * lax.rsqrt(squares - mean * mean + EPS) * gain).astype(jnp.bfloat16)

    all_query, all_keys, all_value = (projected(plane) for plane in range(3))
    for head in range(out_ref.shape[1] // HD):
        cols = slice(head * HD, (head + 1) * HD)
        query = head_norm(all_query[:, cols], qk_gain_ref[0:1, :])
        keys = head_norm(all_keys[:, cols], qk_gain_ref[1:2, :])
        value = all_value[:, cols].astype(jnp.bfloat16)
        scores = lax.dot_general(query, keys, (((1,), (1,)), ((), ())), preferred_element_type=jnp.float32)
        expo = jnp.exp(scores * HD**-0.5)
        attend = (expo * (1.0 / jnp.sum(expo, axis=-1, keepdims=True))).astype(jnp.bfloat16)
        out_ref[:, cols] = jnp.dot(attend, value, preferred_element_type=jnp.float32).astype(jnp.bfloat16)


def partial(rows, late_rows, gain, w_planes, blocks):
    patches, width = blocks[0].shape
    planes, _, cols = w_planes.shape
    count = len(blocks)
    return pl.pallas_call(
        functools.partial(partial_block, count),
        out_shape=[
            jax.ShapeDtypeStruct((planes, patches + EXTRA, cols), jnp.float32),
            jax.ShapeDtypeStruct((2, patches, 128), jnp.float32),
            jax.ShapeDtypeStruct((patches, 128), jnp.float32),
            jax.ShapeDtypeStruct((planes, LATE * width, cols), jnp.bfloat16),
        ],
        in_specs=[SMEM, SMEM, VMEM, pl.BlockSpec(memory_space=pltpu.HBM)] + [VMEM] * count,
        out_specs=[VMEM] * 4,
        scratch_shapes=[
            pltpu.VMEM((patches + EXTRA, count * width), jnp.bfloat16),
            pltpu.VMEM((planes, count * width, cols), jnp.bfloat16),
            pltpu.SemaphoreType.DMA((count,)),
            pltpu.SemaphoreType.DMA((LATE,)),
        ],
        compiler_params=pltpu.CompilerParams(vmem_limit_bytes=28 << 20),
        name="qkv_partial",
    )(rows, late_rows, gain, w_planes, *blocks)


def attention(rows, gain, blocks, carried, qk_gain, pieces):
    patches, width = blocks[0].shape
    cols = carried[0].shape[2]
    count = len(blocks)
    return pl.pallas_call(
        functools.partial(final_block, count, pieces),
        out_shape=jax.ShapeDtypeStruct((patches, cols), jnp.bfloat16),
        in_specs=[SMEM] + [VMEM] * (count + 6),
        out_specs=VMEM,
        scratch_shapes=[
            pltpu.VMEM((2, patches, 128), jnp.float32),
            pltpu.VMEM((patches + EXTRA, count * width), jnp.bfloat16),
        ],
        compiler_params=pltpu.CompilerParams(vmem_limit_bytes=20 << 20),
        name="attention_block",
    )(rows, gain, *blocks, *carried, qk_gain)


def projection_block(places, order_ref, own_ref, other_ref, w_own_ref, w_other_ref, *out_refs):
    width = out_refs[0].shape[1]
    for at, out_ref in zip(places, out_refs):
        in_own = pl.ds(pl.multiple_of((order_ref[0] + order_ref[1 + at]) * width, width), width)
        in_other = pl.ds(pl.multiple_of(order_ref[1 + at] * width, width), width)
        out = jnp.dot(own_ref[...], w_own_ref[:, in_own], preferred_element_type=jnp.float32)
        out += jnp.dot(other_ref[...], w_other_ref[:, in_other], preferred_element_type=jnp.float32)
        out_ref[...] = out.astype(out_ref.dtype)


def projection(order, own, other, w_own, w_other, ring, places):
    shape = (own.shape[0], w_other.shape[1] // ring)
    out = pl.pallas_call(
        functools.partial(projection_block, places),
        out_shape=[jax.ShapeDtypeStruct(shape, jnp.bfloat16)] * len(places),
        in_specs=[SMEM] + [VMEM] * 4,
        out_specs=[VMEM] * len(places),
        compiler_params=pltpu.CompilerParams(vmem_limit_bytes=24 << 20),
        name="projection_block",
    )(order, own, other, w_own, w_other)
    return dict(zip(places, out))


def shifted(block, axis, by):
    peers = lax.axis_size(axis)
    return lax.ppermute(block, axis, [(i, (i + by) % peers) for i in range(peers)])


def turns(section):
    return section % 8 == 7


def to_next_section(block, by):
    sections, ring = lax.axis_size(SECTION), lax.axis_size(RING)

    def place(s, y, z):
        return ((s % sections) * 2 + y) * ring + z % ring

    pairs = [
        (place(s, y, z), place(s + 1, 1 - y if turns(s) else y, z + by))
        for s in range(sections)
        for y in range(2)
        for z in range(ring)
    ]
    return lax.ppermute(block, SECTION + (PAIR, RING), pairs)


def added(*blocks):
    return functools.reduce(jnp.add, (b.astype(jnp.float32) for b in blocks)).astype(jnp.bfloat16)


def on_device(state, ln_gain, w_qkv, qk_gain, w_out):
    ring = lax.axis_size(RING)
    assert ring == 8
    here, side = lax.axis_index(RING), lax.axis_index(PAIR)
    own = state[0]
    width = own.shape[1]
    flip = turns(lax.axis_index(SECTION))
    kept_side = side ^ flip.astype(side.dtype)
    w_planes = pltpu.with_memory_space_constraint(jnp.transpose(w_qkv[0], (1, 0, 2)), pltpu.HBM)
    gain = ln_gain[0].reshape(2 * ring, 1, width)
    w_own = w_out[0]

    def rows(*places):
        return jnp.stack([(side ^ y) * ring + (here + o) % ring for y, o in places]).astype(jnp.int32)

    early_rows = rows(
        (0, 0), (1, 0), *((y, o) for k in (1, 2, 3) for y, o in ((0, -k), (0, k), (1, -k), (1, k)))
    )
    late_rows = rows((0, -4), (1, 4))
    order = jnp.concatenate([kept_side[None] * ring, (here + jnp.arange(ring)) % ring]).astype(jnp.int32)

    half = w_own.shape[1] // 2

    def step(_, own):
        other = shifted(own, PAIR, 1)
        w_give = lax.dynamic_slice_in_dim(lax.optimization_barrier((w_own, own))[0], (1 - kept_side) * half, half, 1)
        w_other = shifted(lax.optimization_barrier((w_give, other))[0], PAIR, 1)
        blocks = [own, other]
        a_up = a_down = own
        b_up = b_down = other
        for _ in range(3):
            a_up, a_down = shifted(a_up, RING, 1), shifted(a_down, RING, -1)
            b_up, b_down = shifted(b_up, RING, 1), shifted(b_down, RING, -1)
            blocks += [a_up, a_down, b_up, b_down]
        late = [shifted(a_up, RING, 1), shifted(b_down, RING, -1)]

        sums = partial(early_rows, late_rows, gain, w_planes, blocks)
        mixed = attention(late_rows, gain, late, sums, qk_gain[0], 2 * ring)
        mixed_other = shifted(mixed, PAIR, 1)
        parts = projection(order, mixed, mixed_other, w_own, w_other, ring, (4,))
        up = shifted(parts[4], RING, 1)
        mixed_other = lax.optimization_barrier((mixed_other, parts[4]))[0]
        parts |= projection(order, mixed, mixed_other, w_own, w_other, ring, (5, 3, 6, 0, 7, 2, 1))
        down = shifted(parts[5], RING, -1)

        kept = to_next_section(added(jnp.where(flip, other, own), parts[0]), 0)
        down = to_next_section(added(shifted(added(down, parts[6]), RING, -1), parts[7]), -1)
        for k in (3, 2):
            up = shifted(added(up, parts[k]), RING, 1)
        up = to_next_section(added(up, parts[1]), 1)
        return added(kept, down, up)

    return lax.fori_loop(0, STEPS, step, own)[None]


def solution(mesh):
    assert dict(mesh.shape) == {"section": 16, "tensor": 16}
    devices = mesh.devices.reshape(2, 4, 2, 2, 8)
    fine = Mesh(devices, SECTION + (PAIR, RING))
    tensor = (PAIR, RING)
    return jax.shard_map(
        on_device,
        mesh=fine,
        in_specs=(
            P(SECTION, None, tensor),
            P(SECTION, None),
            P(SECTION, None, None, tensor),
            P(SECTION, None, None),
            P(SECTION, tensor, None),
        ),
        out_specs=P(SECTION, None, tensor),
        check_vma=False,
    )
```

```python
import functools

import jax
import jax.numpy as jnp
from jax import lax
from jax.experimental import pallas as pl
from jax.experimental.pallas import tpu as pltpu
from jax.sharding import Mesh, PartitionSpec as P

HD = 128
STEPS = 2
EPS = 1e-06
SECTION = ("yh", "x", "core")
PAIR = "yl"
RING = "z"
EXTRA = 16
VMEM = pl.BlockSpec(memory_space=pltpu.VMEM)
SMEM = pl.BlockSpec(memory_space=pltpu.SMEM)
ROWS = 64
GROUP = 4
LATE = 4


def fetches(rows_ref, w_hbm, w_ref, w_sem, count, width):
    def fetch(at):
        start = pl.multiple_of(rows_ref[at] * width, width)
        return pltpu.make_async_copy(
            w_hbm.at[:, pl.ds(start, width), :], w_ref.at[:, pl.ds(at * width, width), :], w_sem.at[at]
        )

    return [fetch(at) for at in range(count)]


def scale_blocks(first, rows_ref, gain_ref, x_refs, before_ref, sums_ref, shift_ref, scaled_ref):
    patches, width = x_refs[0].shape
    for at in range(len(x_refs)):
        gain = gain_ref[rows_ref[at]]
        high = gain.astype(jnp.bfloat16).astype(jnp.float32)
        row = lax.broadcasted_iota(jnp.int32, (EXTRA, width), 0)
        both = jnp.where(row == 0, high, jnp.where(row == 1, gain - high, 0.0))
        scaled_ref[patches : patches + EXTRA, at * width : (at + 1) * width] = both.astype(jnp.bfloat16)

    @pl.loop(0, patches // ROWS)
    def _(block):
        part = pl.ds(pl.multiple_of(block * ROWS, ROWS), ROWS)
        if first:
            shift = jnp.sum(x_refs[0][part, :].astype(jnp.float32), axis=-1, keepdims=True) / width
            shift_ref[part, :] = jnp.broadcast_to(shift, (ROWS, 128))
            total = squares = jnp.zeros((ROWS, 128), jnp.float32)
        else:
            shift = shift_ref[part, 0:1]
            total, squares = before_ref[0, part, :], before_ref[1, part, :]
        for at, x_ref in enumerate(x_refs):
            values = x_ref[part, :].astype(jnp.float32)
            for lane in range(0, width, 128):
                piece = values[:, lane : lane + 128]
                total += piece
                squares += piece * piece
            scaled = (values - shift) * gain_ref[rows_ref[at]]
            scaled_ref[part, at * width : (at + 1) * width] = scaled.astype(jnp.bfloat16)
        sums_ref[0, part, :] = total
        sums_ref[1, part, :] = squares


def partial_block(blocks, rows_ref, late_rows_ref, gain_ref, w_hbm, *refs):
    x_refs, (acc_ref, sums_ref, shift_ref, w_late_ref, scaled_ref, w_ref, w_sem, late_sem) = refs[:blocks], refs[blocks:]
    width = x_refs[0].shape[1]
    now = fetches(rows_ref, w_hbm, w_ref, w_sem, blocks, width)
    late = fetches(late_rows_ref, w_hbm, w_late_ref, late_sem, LATE, width)
    for copy in now + late:
        copy.start()
    scale_blocks(True, rows_ref, gain_ref, x_refs, None, sums_ref, shift_ref, scaled_ref)
    depth = GROUP * width
    for group in range(blocks // GROUP):
        span = slice(group * depth, (group + 1) * depth)
        for copy in now[group * GROUP : (group + 1) * GROUP]:
            copy.wait()

        @pl.loop(0, 3)
        def _(plane):
            out = jnp.dot(scaled_ref[:, span], w_ref[plane, span, :], preferred_element_type=jnp.float32)
            if group == 0:
                acc_ref[plane] = out
            else:
                acc_ref[plane] += out

    for copy in late:
        copy.wait()


def final_block(blocks, pieces, rows_ref, gain_ref, *refs):
    x_refs, (acc_ref, before_ref, shift_ref, w_ref, qk_gain_ref, out_ref, sums_ref, scaled_ref) = (
        refs[:blocks],
        refs[blocks:],
    )
    patches, width = x_refs[0].shape
    full_width = pieces * width
    scale_blocks(False, rows_ref, gain_ref, x_refs, before_ref, sums_ref, shift_ref, scaled_ref)
    mean = jnp.sum(sums_ref[0], axis=-1, keepdims=True) / full_width
    spread = jnp.sum(sums_ref[1], axis=-1, keepdims=True) / full_width - mean * mean
    scale = lax.rsqrt(spread + EPS)
    offset = mean - shift_ref[:, 0:1]

    def projected(plane):
        out = acc_ref[plane] + jnp.dot(scaled_ref[...], w_ref[plane], preferred_element_type=jnp.float32)
        weighed = out[patches : patches + 1] + out[patches + 1 : patches + 2]
        return (out[:patches] - offset * weighed) * scale

    def head_norm(values, gain):
        mean = jnp.mean(values, axis=-1, keepdims=True)
        squares = jnp.mean(values * values, axis=-1, keepdims=True)
        return ((values - mean) * lax.rsqrt(squares - mean * mean + EPS) * gain).astype(jnp.bfloat16)

    all_query, all_keys, all_value = (projected(plane) for plane in range(3))
    for head in range(out_ref.shape[1] // HD):
        cols = slice(head * HD, (head + 1) * HD)
        query = head_norm(all_query[:, cols], qk_gain_ref[0:1, :])
        keys = head_norm(all_keys[:, cols], qk_gain_ref[1:2, :])
        value = all_value[:, cols].astype(jnp.bfloat16)
        scores = lax.dot_general(query, keys, (((1,), (1,)), ((), ())), preferred_element_type=jnp.float32)
        expo = jnp.exp(scores * HD**-0.5)
        attend = (expo * (1.0 / jnp.sum(expo, axis=-1, keepdims=True))).astype(jnp.bfloat16)
        out_ref[:, cols] = jnp.dot(attend, value, preferred_element_type=jnp.float32).astype(jnp.bfloat16)


def partial(rows, late_rows, gain, w_planes, blocks):
    patches, width = blocks[0].shape
    planes, _, cols = w_planes.shape
    count = len(blocks)
    return pl.pallas_call(
        functools.partial(partial_block, count),
        out_shape=[
            jax.ShapeDtypeStruct((planes, patches + EXTRA, cols), jnp.float32),
            jax.ShapeDtypeStruct((2, patches, 128), jnp.float32),
            jax.ShapeDtypeStruct((patches, 128), jnp.float32),
            jax.ShapeDtypeStruct((planes, LATE * width, cols), jnp.bfloat16),
        ],
        in_specs=[SMEM, SMEM, VMEM, pl.BlockSpec(memory_space=pltpu.HBM)] + [VMEM] * count,
        out_specs=[VMEM] * 4,
        scratch_shapes=[
            pltpu.VMEM((patches + EXTRA, count * width), jnp.bfloat16),
            pltpu.VMEM((planes, count * width, cols), jnp.bfloat16),
            pltpu.SemaphoreType.DMA((count,)),
            pltpu.SemaphoreType.DMA((LATE,)),
        ],
        compiler_params=pltpu.CompilerParams(vmem_limit_bytes=28 << 20),
        name="qkv_partial",
    )(rows, late_rows, gain, w_planes, *blocks)


def attention(rows, gain, blocks, carried, qk_gain, pieces):
    patches, width = blocks[0].shape
    cols = carried[0].shape[2]
    count = len(blocks)
    return pl.pallas_call(
        functools.partial(final_block, count, pieces),
        out_shape=jax.ShapeDtypeStruct((patches, cols), jnp.bfloat16),
        in_specs=[SMEM] + [VMEM] * (count + 6),
        out_specs=VMEM,
        scratch_shapes=[
            pltpu.VMEM((2, patches, 128), jnp.float32),
            pltpu.VMEM((patches + EXTRA, count * width), jnp.bfloat16),
        ],
        compiler_params=pltpu.CompilerParams(vmem_limit_bytes=20 << 20),
        name="attention_block",
    )(rows, gain, *blocks, *carried, qk_gain)


def projection_block(places, order_ref, own_ref, other_ref, w_own_ref, w_other_ref, *out_refs):
    width = out_refs[0].shape[1]
    for at, out_ref in zip(places, out_refs):
        in_own = pl.ds(pl.multiple_of((order_ref[0] + order_ref[1 + at]) * width, width), width)
        in_other = pl.ds(pl.multiple_of(order_ref[1 + at] * width, width), width)
        out = jnp.dot(own_ref[...], w_own_ref[:, in_own], preferred_element_type=jnp.float32)
        out += jnp.dot(other_ref[...], w_other_ref[:, in_other], preferred_element_type=jnp.float32)
        out_ref[...] = out.astype(out_ref.dtype)


def projection(order, own, other, w_own, w_other, ring, places):
    shape = (own.shape[0], w_other.shape[1] // ring)
    out = pl.pallas_call(
        functools.partial(projection_block, places),
        out_shape=[jax.ShapeDtypeStruct(shape, jnp.bfloat16)] * len(places),
        in_specs=[SMEM] + [VMEM] * 4,
        out_specs=[VMEM] * len(places),
        compiler_params=pltpu.CompilerParams(vmem_limit_bytes=24 << 20),
        name="projection_block",
    )(order, own, other, w_own, w_other)
    return dict(zip(places, out))


def shifted(block, axis, by):
    peers = lax.axis_size(axis)
    return lax.ppermute(block, axis, [(i, (i + by) % peers) for i in range(peers)])


def across(block, by):
    ring = lax.axis_size(RING)
    pairs = [(y * ring + z, (1 - y) * ring + (z + by) % ring) for y in range(2) for z in range(ring)]
    return lax.ppermute(block, (PAIR, RING), pairs)


def turns(section):
    return section % 8 == 7


def to_next_section(block, by):
    sections, ring = lax.axis_size(SECTION), lax.axis_size(RING)

    def place(s, y, z):
        return ((s % sections) * 2 + y) * ring + z % ring

    pairs = [
        (place(s, y, z), place(s + 1, 1 - y if turns(s) else y, z + by))
        for s in range(sections)
        for y in range(2)
        for z in range(ring)
    ]
    return lax.ppermute(block, SECTION + (PAIR, RING), pairs)


def added(*blocks):
    return functools.reduce(jnp.add, (b.astype(jnp.float32) for b in blocks)).astype(jnp.bfloat16)


def on_device(state, ln_gain, w_qkv, qk_gain, w_out):
    ring = lax.axis_size(RING)
    assert ring == 8
    here, side = lax.axis_index(RING), lax.axis_index(PAIR)
    own = state[0]
    width = own.shape[1]
    flip = turns(lax.axis_index(SECTION))
    kept_side = side ^ flip.astype(side.dtype)
    w_planes = pltpu.with_memory_space_constraint(jnp.transpose(w_qkv[0], (1, 0, 2)), pltpu.HBM)
    gain = ln_gain[0].reshape(2 * ring, 1, width)
    w_own = w_out[0]

    def rows(*places):
        return jnp.stack([(side ^ y) * ring + (here + o) % ring for y, o in places]).astype(jnp.int32)

    early_rows = rows(
        (0, 0), (1, 0), (0, -1), (0, 1), (0, -2), (0, 2), (1, -1), (1, 1), (0, -3), (0, 3), (1, -2), (1, 2)
    )
    late_rows = rows((0, -4), (1, -3), (1, 3), (1, 4))
    order = jnp.concatenate([kept_side[None] * ring, (here + jnp.arange(ring)) % ring]).astype(jnp.int32)

    half = w_own.shape[1] // 2

    def step(_, own):
        a_up, a_down = shifted(own, RING, 1), shifted(own, RING, -1)
        other = shifted(own, PAIR, 1)
        a_up, a_down, other = lax.optimization_barrier((a_up, a_down, other))
        w_give = lax.dynamic_slice_in_dim(lax.optimization_barrier((w_own, own))[0], (1 - kept_side) * half, half, 1)
        w_other = shifted(lax.optimization_barrier((w_give, other))[0], PAIR, 1)
        blocks = [own, other, a_up, a_down]
        b_up = b_down = other
        for _ in range(2):
            a_up, a_down = shifted(a_up, RING, 1), shifted(a_down, RING, -1)
            b_up, b_down = shifted(b_up, RING, 1), shifted(b_down, RING, -1)
            blocks += [a_up, a_down, b_up, b_down]
        late = [shifted(a_up, RING, 1), shifted(b_up, RING, 1), shifted(b_down, RING, -1), across(a_down, -1)]

        sums = partial(early_rows, late_rows, gain, w_planes, blocks)
        mixed = attention(late_rows, gain, late, sums, qk_gain[0], 2 * ring)
        mixed_other = shifted(mixed, PAIR, 1)
        parts = projection(order, mixed, mixed_other, w_own, w_other, ring, (4,))
        up = shifted(parts[4], RING, 1)
        mixed_other = lax.optimization_barrier((mixed_other, parts[4]))[0]
        parts |= projection(order, mixed, mixed_other, w_own, w_other, ring, (5, 3, 6, 0, 7, 2, 1))
        down = shifted(parts[5], RING, -1)

        kept = to_next_section(added(jnp.where(flip, other, own), parts[0]), 0)
        down = to_next_section(added(shifted(added(down, parts[6]), RING, -1), parts[7]), -1)
        for k in (3, 2):
            up = shifted(added(up, parts[k]), RING, 1)
        up = to_next_section(added(up, parts[1]), 1)
        return added(kept, down, up)

    return lax.fori_loop(0, STEPS, step, own)[None]


def solution(mesh):
    assert dict(mesh.shape) == {"section": 16, "tensor": 16}
    devices = mesh.devices.reshape(2, 4, 2, 2, 8)
    fine = Mesh(devices, SECTION + (PAIR, RING))
    tensor = (PAIR, RING)
    return jax.shard_map(
        on_device,
        mesh=fine,
        in_specs=(
            P(SECTION, None, tensor),
            P(SECTION, None),
            P(SECTION, None, None, tensor),
            P(SECTION, None, None),
            P(SECTION, tensor, None),
        ),
        out_specs=P(SECTION, None, tensor),
        check_vma=False,
    )
```

```python
import functools

import jax
import jax.numpy as jnp
from jax import lax
from jax.experimental import pallas as pl
from jax.experimental.pallas import tpu as pltpu
from jax.sharding import Mesh, PartitionSpec as P

HD = 128
STEPS = 2
EPS = 1e-06
SECTION = ("yh", "x", "core")
PAIR = "yl"
RING = "z"
EXTRA = 16
VMEM = pl.BlockSpec(memory_space=pltpu.VMEM)
SMEM = pl.BlockSpec(memory_space=pltpu.SMEM)
ROWS = 64
GROUP = 4
LATE = 4


def fetches(rows_ref, w_hbm, w_ref, w_sem, count, width):
    def fetch(at):
        start = pl.multiple_of(rows_ref[at] * width, width)
        return pltpu.make_async_copy(
            w_hbm.at[:, pl.ds(start, width), :], w_ref.at[:, pl.ds(at * width, width), :], w_sem.at[at]
        )

    return [fetch(at) for at in range(count)]


def scale_blocks(first, rows_ref, gain_ref, x_refs, before_ref, sums_ref, shift_ref, scaled_ref):
    patches, width = x_refs[0].shape
    for at in range(len(x_refs)):
        gain = gain_ref[rows_ref[at]]
        high = gain.astype(jnp.bfloat16).astype(jnp.float32)
        row = lax.broadcasted_iota(jnp.int32, (EXTRA, width), 0)
        both = jnp.where(row == 0, high, jnp.where(row == 1, gain - high, 0.0))
        scaled_ref[patches : patches + EXTRA, at * width : (at + 1) * width] = both.astype(jnp.bfloat16)

    @pl.loop(0, patches // ROWS)
    def _(block):
        part = pl.ds(pl.multiple_of(block * ROWS, ROWS), ROWS)
        if first:
            shift = jnp.sum(x_refs[0][part, :].astype(jnp.float32), axis=-1, keepdims=True) / width
            shift_ref[part, :] = jnp.broadcast_to(shift, (ROWS, 128))
            total = squares = jnp.zeros((ROWS, 128), jnp.float32)
        else:
            shift = shift_ref[part, 0:1]
            total, squares = before_ref[0, part, :], before_ref[1, part, :]
        for at, x_ref in enumerate(x_refs):
            values = x_ref[part, :].astype(jnp.float32)
            for lane in range(0, width, 128):
                piece = values[:, lane : lane + 128]
                total += piece
                squares += piece * piece
            scaled = (values - shift) * gain_ref[rows_ref[at]]
            scaled_ref[part, at * width : (at + 1) * width] = scaled.astype(jnp.bfloat16)
        sums_ref[0, part, :] = total
        sums_ref[1, part, :] = squares


def partial_block(blocks, rows_ref, late_rows_ref, gain_ref, w_hbm, *refs):
    x_refs, (acc_ref, sums_ref, shift_ref, w_late_ref, scaled_ref, w_ref, w_sem, late_sem) = refs[:blocks], refs[blocks:]
    width = x_refs[0].shape[1]
    now = fetches(rows_ref, w_hbm, w_ref, w_sem, blocks, width)
    late = fetches(late_rows_ref, w_hbm, w_late_ref, late_sem, LATE, width)
    for copy in now + late:
        copy.start()
    scale_blocks(True, rows_ref, gain_ref, x_refs, None, sums_ref, shift_ref, scaled_ref)
    depth = GROUP * width
    for group in range(blocks // GROUP):
        span = slice(group * depth, (group + 1) * depth)
        for copy in now[group * GROUP : (group + 1) * GROUP]:
            copy.wait()

        @pl.loop(0, 3)
        def _(plane):
            out = jnp.dot(scaled_ref[:, span], w_ref[plane, span, :], preferred_element_type=jnp.float32)
            if group == 0:
                acc_ref[plane] = out
            else:
                acc_ref[plane] += out

    for copy in late:
        copy.wait()


def final_block(blocks, pieces, rows_ref, gain_ref, *refs):
    x_refs, (acc_ref, before_ref, shift_ref, w_ref, qk_gain_ref, out_ref, sums_ref, scaled_ref) = (
        refs[:blocks],
        refs[blocks:],
    )
    patches, width = x_refs[0].shape
    full_width = pieces * width
    scale_blocks(False, rows_ref, gain_ref, x_refs, before_ref, sums_ref, shift_ref, scaled_ref)
    mean = jnp.sum(sums_ref[0], axis=-1, keepdims=True) / full_width
    spread = jnp.sum(sums_ref[1], axis=-1, keepdims=True) / full_width - mean * mean
    scale = lax.rsqrt(spread + EPS)
    offset = mean - shift_ref[:, 0:1]

    def projected(plane):
        out = acc_ref[plane] + jnp.dot(scaled_ref[...], w_ref[plane], preferred_element_type=jnp.float32)
        weighed = out[patches : patches + 1] + out[patches + 1 : patches + 2]
        return (out[:patches] - offset * weighed) * scale

    def head_norm(values, gain):
        mean = jnp.mean(values, axis=-1, keepdims=True)
        squares = jnp.mean(values * values, axis=-1, keepdims=True)
        return ((values - mean) * lax.rsqrt(squares - mean * mean + EPS) * gain).astype(jnp.bfloat16)

    all_query, all_keys, all_value = (projected(plane) for plane in range(3))
    for head in range(out_ref.shape[1] // HD):
        cols = slice(head * HD, (head + 1) * HD)
        query = head_norm(all_query[:, cols], qk_gain_ref[0:1, :])
        keys = head_norm(all_keys[:, cols], qk_gain_ref[1:2, :])
        value = all_value[:, cols].astype(jnp.bfloat16)
        scores = lax.dot_general(query, keys, (((1,), (1,)), ((), ())), preferred_element_type=jnp.float32)
        expo = jnp.exp(scores * HD**-0.5)
        attend = (expo * (1.0 / jnp.sum(expo, axis=-1, keepdims=True))).astype(jnp.bfloat16)
        out_ref[:, cols] = jnp.dot(attend, value, preferred_element_type=jnp.float32).astype(jnp.bfloat16)


def partial(rows, late_rows, gain, w_planes, blocks):
    patches, width = blocks[0].shape
    planes, _, cols = w_planes.shape
    count = len(blocks)
    return pl.pallas_call(
        functools.partial(partial_block, count),
        out_shape=[
            jax.ShapeDtypeStruct((planes, patches + EXTRA, cols), jnp.float32),
            jax.ShapeDtypeStruct((2, patches, 128), jnp.float32),
            jax.ShapeDtypeStruct((patches, 128), jnp.float32),
            jax.ShapeDtypeStruct((planes, LATE * width, cols), jnp.bfloat16),
        ],
        in_specs=[SMEM, SMEM, VMEM, pl.BlockSpec(memory_space=pltpu.HBM)] + [VMEM] * count,
        out_specs=[VMEM] * 4,
        scratch_shapes=[
            pltpu.VMEM((patches + EXTRA, count * width), jnp.bfloat16),
            pltpu.VMEM((planes, count * width, cols), jnp.bfloat16),
            pltpu.SemaphoreType.DMA((count,)),
            pltpu.SemaphoreType.DMA((LATE,)),
        ],
        compiler_params=pltpu.CompilerParams(vmem_limit_bytes=28 << 20),
        name="qkv_partial",
    )(rows, late_rows, gain, w_planes, *blocks)


def attention(rows, gain, blocks, carried, qk_gain, pieces):
    patches, width = blocks[0].shape
    cols = carried[0].shape[2]
    count = len(blocks)
    return pl.pallas_call(
        functools.partial(final_block, count, pieces),
        out_shape=jax.ShapeDtypeStruct((patches, cols), jnp.bfloat16),
        in_specs=[SMEM] + [VMEM] * (count + 6),
        out_specs=VMEM,
        scratch_shapes=[
            pltpu.VMEM((2, patches, 128), jnp.float32),
            pltpu.VMEM((patches + EXTRA, count * width), jnp.bfloat16),
        ],
        compiler_params=pltpu.CompilerParams(vmem_limit_bytes=20 << 20),
        name="attention_block",
    )(rows, gain, *blocks, *carried, qk_gain)


def projection_block(places, order_ref, own_ref, other_ref, w_own_ref, w_other_ref, *out_refs):
    width = out_refs[0].shape[1]
    for at, out_ref in zip(places, out_refs):
        in_own = pl.ds(pl.multiple_of((order_ref[0] + order_ref[1 + at]) * width, width), width)
        in_other = pl.ds(pl.multiple_of(order_ref[1 + at] * width, width), width)
        out = jnp.dot(own_ref[...], w_own_ref[:, in_own], preferred_element_type=jnp.float32)
        out += jnp.dot(other_ref[...], w_other_ref[:, in_other], preferred_element_type=jnp.float32)
        out_ref[...] = out.astype(out_ref.dtype)


def projection(order, own, other, w_own, w_other, ring, places):
    shape = (own.shape[0], w_other.shape[1] // ring)
    out = pl.pallas_call(
        functools.partial(projection_block, places),
        out_shape=[jax.ShapeDtypeStruct(shape, jnp.bfloat16)] * len(places),
        in_specs=[SMEM] + [VMEM] * 4,
        out_specs=[VMEM] * len(places),
        compiler_params=pltpu.CompilerParams(vmem_limit_bytes=24 << 20),
        name="projection_block",
    )(order, own, other, w_own, w_other)
    return dict(zip(places, out))


def shifted(block, axis, by):
    peers = lax.axis_size(axis)
    return lax.ppermute(block, axis, [(i, (i + by) % peers) for i in range(peers)])


def across(block, by):
    ring = lax.axis_size(RING)
    pairs = [(y * ring + z, (1 - y) * ring + (z + by) % ring) for y in range(2) for z in range(ring)]
    return lax.ppermute(block, (PAIR, RING), pairs)


def turns(section):
    return section % 8 == 7


def to_next_section(block, by):
    sections, ring = lax.axis_size(SECTION), lax.axis_size(RING)

    def place(s, y, z):
        return ((s % sections) * 2 + y) * ring + z % ring

    pairs = [
        (place(s, y, z), place(s + 1, 1 - y if turns(s) else y, z + by))
        for s in range(sections)
        for y in range(2)
        for z in range(ring)
    ]
    return lax.ppermute(block, SECTION + (PAIR, RING), pairs)


def added(*blocks):
    return functools.reduce(jnp.add, (b.astype(jnp.float32) for b in blocks)).astype(jnp.bfloat16)


def on_device(state, ln_gain, w_qkv, qk_gain, w_out):
    ring = lax.axis_size(RING)
    assert ring == 8
    here, side = lax.axis_index(RING), lax.axis_index(PAIR)
    own = state[0]
    width = own.shape[1]
    flip = turns(lax.axis_index(SECTION))
    kept_side = side ^ flip.astype(side.dtype)
    w_planes = pltpu.with_memory_space_constraint(jnp.transpose(w_qkv[0], (1, 0, 2)), pltpu.HBM)
    gain = ln_gain[0].reshape(2 * ring, 1, width)
    w_own = w_out[0]

    def rows(*places):
        return jnp.stack([(side ^ y) * ring + (here + o) % ring for y, o in places]).astype(jnp.int32)

    early_rows = rows(
        (0, 0), (1, 0), (0, -1), (0, 1), (0, -2), (0, 2), (1, -1), (1, 1), (0, -3), (0, 3), (1, -2), (1, 2)
    )
    late_rows = rows((0, -4), (1, -3), (1, 3), (1, 4))
    order = jnp.concatenate([kept_side[None] * ring, (here + jnp.arange(ring)) % ring]).astype(jnp.int32)

    half = w_own.shape[1] // 2

    def step(_, own):
        a_up, a_down = shifted(own, RING, 1), shifted(own, RING, -1)
        other = shifted(own, PAIR, 1)
        a_up, a_down, other = lax.optimization_barrier((a_up, a_down, other))
        w_give = lax.dynamic_slice_in_dim(lax.optimization_barrier((w_own, own))[0], (1 - kept_side) * half, half, 1)
        w_other = shifted(lax.optimization_barrier((w_give, other))[0], PAIR, 1)
        blocks = [own, other, a_up, a_down]
        b_up = b_down = other
        for _ in range(2):
            a_up, a_down = shifted(a_up, RING, 1), shifted(a_down, RING, -1)
            b_up, b_down = shifted(b_up, RING, 1), shifted(b_down, RING, -1)
            blocks += [a_up, a_down, b_up, b_down]
        late = [shifted(a_up, RING, 1), shifted(b_up, RING, 1), shifted(b_down, RING, -1), across(a_down, -1)]

        sums = partial(early_rows, late_rows, gain, w_planes, blocks)
        mixed = attention(late_rows, gain, late, sums, qk_gain[0], 2 * ring)
        mixed_other = shifted(mixed, PAIR, 1)
        parts = projection(order, mixed, mixed_other, w_own, w_other, ring, (4, 5))
        up, down = shifted(parts[4], RING, 1), shifted(parts[5], RING, -1)
        parts |= projection(order, mixed, mixed_other, w_own, w_other, ring, (3, 6, 2, 7, 1, 0))

        for k in (3, 2):
            up = shifted(added(up, parts[k]), RING, 1)
            down = shifted(added(down, parts[9 - k]), RING, -1)
        up = to_next_section(added(up, parts[1]), 1)
        own = to_next_section(added(jnp.where(flip, other, own), down, parts[0]), 0)
        return added(own, up)

    return lax.fori_loop(0, STEPS, step, own)[None]


def solution(mesh):
    assert dict(mesh.shape) == {"section": 16, "tensor": 16}
    devices = mesh.devices.reshape(2, 4, 2, 2, 8)
    fine = Mesh(devices, SECTION + (PAIR, RING))
    tensor = (PAIR, RING)
    return jax.shard_map(
        on_device,
        mesh=fine,
        in_specs=(
            P(SECTION, None, tensor),
            P(SECTION, None),
            P(SECTION, None, None, tensor),
            P(SECTION, None, None),
            P(SECTION, tensor, None),
        ),
        out_specs=P(SECTION, None, tensor),
        check_vma=False,
    )
```

```python
import functools

import jax
import jax.numpy as jnp
from jax import lax
from jax.experimental import pallas as pl
from jax.experimental.pallas import tpu as pltpu
from jax.sharding import Mesh, PartitionSpec as P

HD = 128
STEPS = 2
EPS = 1e-06
SECTION = ("yh", "x", "core")
PAIR = "yl"
RING = "z"
EXTRA = 16
VMEM = pl.BlockSpec(memory_space=pltpu.VMEM)
SMEM = pl.BlockSpec(memory_space=pltpu.SMEM)
ROWS = 64
GROUP = 4
LATE = 4


def fetches(rows_ref, w_hbm, w_ref, w_sem, count, width):
    def fetch(at):
        start = pl.multiple_of(rows_ref[at] * width, width)
        return pltpu.make_async_copy(
            w_hbm.at[:, pl.ds(start, width), :], w_ref.at[:, pl.ds(at * width, width), :], w_sem.at[at]
        )

    return [fetch(at) for at in range(count)]


def scale_blocks(first, rows_ref, gain_ref, x_refs, before_ref, sums_ref, shift_ref, scaled_ref):
    patches, width = x_refs[0].shape
    for at in range(len(x_refs)):
        gain = gain_ref[rows_ref[at]]
        high = gain.astype(jnp.bfloat16).astype(jnp.float32)
        row = lax.broadcasted_iota(jnp.int32, (EXTRA, width), 0)
        both = jnp.where(row == 0, high, jnp.where(row == 1, gain - high, 0.0))
        scaled_ref[patches : patches + EXTRA, at * width : (at + 1) * width] = both.astype(jnp.bfloat16)

    height = ROWS if first else patches

    @pl.loop(0, patches // height)
    def _(block):
        part = pl.ds(pl.multiple_of(block * height, height), height)
        if first:
            shift = jnp.sum(x_refs[0][part, :].astype(jnp.float32), axis=-1, keepdims=True) / width
            shift_ref[part, :] = jnp.broadcast_to(shift, (height, 128))
            total = squares = jnp.zeros((height, 128), jnp.float32)
        else:
            shift = shift_ref[part, 0:1]
            total, squares = before_ref[0, part, :], before_ref[1, part, :]
        for at, x_ref in enumerate(x_refs):
            values = x_ref[part, :].astype(jnp.float32)
            for lane in range(0, width, 128):
                piece = values[:, lane : lane + 128]
                total += piece
                squares += piece * piece
            scaled = (values - shift) * gain_ref[rows_ref[at]]
            scaled_ref[part, at * width : (at + 1) * width] = scaled.astype(jnp.bfloat16)
        sums_ref[0, part, :] = total
        sums_ref[1, part, :] = squares


def partial_block(blocks, rows_ref, late_rows_ref, gain_ref, w_hbm, *refs):
    x_refs, (acc_ref, sums_ref, shift_ref, w_late_ref, scaled_ref, w_ref, w_sem, late_sem) = refs[:blocks], refs[blocks:]
    width = x_refs[0].shape[1]
    now = fetches(rows_ref, w_hbm, w_ref, w_sem, blocks, width)
    late = fetches(late_rows_ref, w_hbm, w_late_ref, late_sem, LATE, width)
    for copy in now + late:
        copy.start()
    scale_blocks(True, rows_ref, gain_ref, x_refs, None, sums_ref, shift_ref, scaled_ref)
    depth = GROUP * width
    for group in range(blocks // GROUP):
        span = slice(group * depth, (group + 1) * depth)
        for copy in now[group * GROUP : (group + 1) * GROUP]:
            copy.wait()

        @pl.loop(0, 3)
        def _(plane):
            out = jnp.dot(scaled_ref[:, span], w_ref[plane, span, :], preferred_element_type=jnp.float32)
            if group == 0:
                acc_ref[plane] = out
            else:
                acc_ref[plane] += out

    for copy in late:
        copy.wait()


def final_block(blocks, pieces, rows_ref, gain_ref, *refs):
    x_refs, (acc_ref, before_ref, shift_ref, w_ref, qk_gain_ref, out_ref, sums_ref, scaled_ref) = (
        refs[:blocks],
        refs[blocks:],
    )
    patches, width = x_refs[0].shape
    full_width = pieces * width
    scale_blocks(False, rows_ref, gain_ref, x_refs, before_ref, sums_ref, shift_ref, scaled_ref)
    mean = jnp.sum(sums_ref[0], axis=-1, keepdims=True) / full_width
    spread = jnp.sum(sums_ref[1], axis=-1, keepdims=True) / full_width - mean * mean
    scale = lax.rsqrt(spread + EPS)
    offset = mean - shift_ref[:, 0:1]

    def projected(plane):
        out = acc_ref[plane] + jnp.dot(scaled_ref[...], w_ref[plane], preferred_element_type=jnp.float32)
        weighed = out[patches : patches + 1] + out[patches + 1 : patches + 2]
        return (out[:patches] - offset * weighed) * scale

    def head_norm(values, gain):
        mean = jnp.mean(values, axis=-1, keepdims=True)
        squares = jnp.mean(values * values, axis=-1, keepdims=True)
        return ((values - mean) * lax.rsqrt(squares - mean * mean + EPS) * gain).astype(jnp.bfloat16)

    all_query, all_keys, all_value = (projected(plane) for plane in range(3))
    for head in range(out_ref.shape[1] // HD):
        cols = slice(head * HD, (head + 1) * HD)
        query = head_norm(all_query[:, cols], qk_gain_ref[0:1, :])
        keys = head_norm(all_keys[:, cols], qk_gain_ref[1:2, :])
        value = all_value[:, cols].astype(jnp.bfloat16)
        scores = lax.dot_general(query, keys, (((1,), (1,)), ((), ())), preferred_element_type=jnp.float32)
        expo = jnp.exp(scores * HD**-0.5)
        attend = (expo * (1.0 / jnp.sum(expo, axis=-1, keepdims=True))).astype(jnp.bfloat16)
        out_ref[:, cols] = jnp.dot(attend, value, preferred_element_type=jnp.float32).astype(jnp.bfloat16)


def partial(rows, late_rows, gain, w_planes, blocks):
    patches, width = blocks[0].shape
    planes, _, cols = w_planes.shape
    count = len(blocks)
    return pl.pallas_call(
        functools.partial(partial_block, count),
        out_shape=[
            jax.ShapeDtypeStruct((planes, patches + EXTRA, cols), jnp.float32),
            jax.ShapeDtypeStruct((2, patches, 128), jnp.float32),
            jax.ShapeDtypeStruct((patches, 128), jnp.float32),
            jax.ShapeDtypeStruct((planes, LATE * width, cols), jnp.bfloat16),
        ],
        in_specs=[SMEM, SMEM, VMEM, pl.BlockSpec(memory_space=pltpu.HBM)] + [VMEM] * count,
        out_specs=[VMEM] * 4,
        scratch_shapes=[
            pltpu.VMEM((patches + EXTRA, count * width), jnp.bfloat16),
            pltpu.VMEM((planes, count * width, cols), jnp.bfloat16),
            pltpu.SemaphoreType.DMA((count,)),
            pltpu.SemaphoreType.DMA((LATE,)),
        ],
        compiler_params=pltpu.CompilerParams(vmem_limit_bytes=28 << 20),
        name="qkv_partial",
    )(rows, late_rows, gain, w_planes, *blocks)


def attention(rows, gain, blocks, carried, qk_gain, pieces):
    patches, width = blocks[0].shape
    cols = carried[0].shape[2]
    count = len(blocks)
    return pl.pallas_call(
        functools.partial(final_block, count, pieces),
        out_shape=jax.ShapeDtypeStruct((patches, cols), jnp.bfloat16),
        in_specs=[SMEM] + [VMEM] * (count + 6),
        out_specs=VMEM,
        scratch_shapes=[
            pltpu.VMEM((2, patches, 128), jnp.float32),
            pltpu.VMEM((patches + EXTRA, count * width), jnp.bfloat16),
        ],
        compiler_params=pltpu.CompilerParams(vmem_limit_bytes=20 << 20),
        name="attention_block",
    )(rows, gain, *blocks, *carried, qk_gain)


def projection_block(places, order_ref, own_ref, other_ref, w_own_ref, w_other_ref, *out_refs):
    width = out_refs[0].shape[1]
    for at, out_ref in zip(places, out_refs):
        in_own = pl.ds(pl.multiple_of((order_ref[0] + order_ref[1 + at]) * width, width), width)
        in_other = pl.ds(pl.multiple_of(order_ref[1 + at] * width, width), width)
        out = jnp.dot(own_ref[...], w_own_ref[:, in_own], preferred_element_type=jnp.float32)
        out += jnp.dot(other_ref[...], w_other_ref[:, in_other], preferred_element_type=jnp.float32)
        out_ref[...] = out.astype(out_ref.dtype)


def projection(order, own, other, w_own, w_other, ring, places):
    shape = (own.shape[0], w_other.shape[1] // ring)
    out = pl.pallas_call(
        functools.partial(projection_block, places),
        out_shape=[jax.ShapeDtypeStruct(shape, jnp.bfloat16)] * len(places),
        in_specs=[SMEM] + [VMEM] * 4,
        out_specs=[VMEM] * len(places),
        compiler_params=pltpu.CompilerParams(vmem_limit_bytes=24 << 20),
        name="projection_block",
    )(order, own, other, w_own, w_other)
    return dict(zip(places, out))


def shifted(block, axis, by):
    peers = lax.axis_size(axis)
    return lax.ppermute(block, axis, [(i, (i + by) % peers) for i in range(peers)])


def across(block, by):
    ring = lax.axis_size(RING)
    pairs = [(y * ring + z, (1 - y) * ring + (z + by) % ring) for y in range(2) for z in range(ring)]
    return lax.ppermute(block, (PAIR, RING), pairs)


def turns(section):
    return section % 8 == 7


def to_next_section(block, by):
    sections, ring = lax.axis_size(SECTION), lax.axis_size(RING)

    def place(s, y, z):
        return ((s % sections) * 2 + y) * ring + z % ring

    pairs = [
        (place(s, y, z), place(s + 1, 1 - y if turns(s) else y, z + by))
        for s in range(sections)
        for y in range(2)
        for z in range(ring)
    ]
    return lax.ppermute(block, SECTION + (PAIR, RING), pairs)


def added(*blocks):
    return functools.reduce(jnp.add, (b.astype(jnp.float32) for b in blocks)).astype(jnp.bfloat16)


def on_device(state, ln_gain, w_qkv, qk_gain, w_out):
    ring = lax.axis_size(RING)
    assert ring == 8
    here, side = lax.axis_index(RING), lax.axis_index(PAIR)
    own = state[0]
    width = own.shape[1]
    flip = turns(lax.axis_index(SECTION))
    kept_side = side ^ flip.astype(side.dtype)
    w_planes = pltpu.with_memory_space_constraint(jnp.transpose(w_qkv[0], (1, 0, 2)), pltpu.HBM)
    gain = ln_gain[0].reshape(2 * ring, 1, width)
    w_own = w_out[0]

    def rows(*places):
        return jnp.stack([(side ^ y) * ring + (here + o) % ring for y, o in places]).astype(jnp.int32)

    early_rows = rows(
        (0, 0), (1, 0), (0, -1), (0, 1), (0, -2), (0, 2), (1, -1), (1, 1), (0, -3), (0, 3), (1, -2), (1, 2)
    )
    late_rows = rows((0, -4), (1, -3), (1, 3), (1, 4))
    order = jnp.concatenate([kept_side[None] * ring, (here + jnp.arange(ring)) % ring]).astype(jnp.int32)

    half = w_own.shape[1] // 2

    def step(_, own):
        a_up, a_down = shifted(own, RING, 1), shifted(own, RING, -1)
        other = shifted(own, PAIR, 1)
        a_up, a_down, other = lax.optimization_barrier((a_up, a_down, other))
        w_give = lax.dynamic_slice_in_dim(lax.optimization_barrier((w_own, own))[0], (1 - kept_side) * half, half, 1)
        w_other = shifted(lax.optimization_barrier((w_give, other))[0], PAIR, 1)
        blocks = [own, other, a_up, a_down]
        b_up = b_down = other
        for _ in range(2):
            a_up, a_down = shifted(a_up, RING, 1), shifted(a_down, RING, -1)
            b_up, b_down = shifted(b_up, RING, 1), shifted(b_down, RING, -1)
            blocks += [a_up, a_down, b_up, b_down]
        late = [shifted(a_up, RING, 1), shifted(b_up, RING, 1), shifted(b_down, RING, -1), across(a_down, -1)]

        sums = partial(early_rows, late_rows, gain, w_planes, blocks)
        mixed = attention(late_rows, gain, late, sums, qk_gain[0], 2 * ring)
        mixed_other = shifted(mixed, PAIR, 1)
        parts = projection(order, mixed, mixed_other, w_own, w_other, ring, (4,))
        up = shifted(parts[4], RING, 1)
        mixed_other = lax.optimization_barrier((mixed_other, parts[4]))[0]
        parts |= projection(order, mixed, mixed_other, w_own, w_other, ring, (5, 3, 6, 0, 7, 2, 1))
        down = shifted(parts[5], RING, -1)

        kept = to_next_section(added(jnp.where(flip, other, own), parts[0]), 0)
        down = to_next_section(added(shifted(added(down, parts[6]), RING, -1), parts[7]), -1)
        for k in (3, 2):
            up = shifted(added(up, parts[k]), RING, 1)
        up = to_next_section(added(up, parts[1]), 1)
        return added(kept, down, up)

    return lax.fori_loop(0, STEPS, step, own)[None]


def solution(mesh):
    assert dict(mesh.shape) == {"section": 16, "tensor": 16}
    devices = mesh.devices.reshape(2, 4, 2, 2, 8)
    fine = Mesh(devices, SECTION + (PAIR, RING))
    tensor = (PAIR, RING)
    return jax.shard_map(
        on_device,
        mesh=fine,
        in_specs=(
            P(SECTION, None, tensor),
            P(SECTION, None),
            P(SECTION, None, None, tensor),
            P(SECTION, None, None),
            P(SECTION, tensor, None),
        ),
        out_specs=P(SECTION, None, tensor),
        check_vma=False,
    )
```
